128 devices in a mesh: walk: 8 (over x, z_lo), pair: 16 (over y, z_hi, core).
Axes of the slice: x: 4, y: 4, z: 4 (z_hi: 2, z_lo: 2; z = z_hi * 2 + z_lo), core: 2. Of those that a mesh axis runs over, the one named last changes fastest.
Arguments:
- walkers: float32 [256, 64, 512], P(('walk', 'pair')), may hold values from -6 to 6
- inverse_intersection: float32 [256, 64, 64], P(('walk', 'pair')), may hold values from -0.75 to 0.75
- trial: bfloat16 [64, 512], P(None, 'walk'), may hold values from -0.095703125 to 0.095703125
- fields: float32 [256, 4096], P(('walk', 'pair')), may hold values from -6 to 6
- cholesky: bfloat16 [512, 512, 4096], P('pair', 'walk'), may hold values from -0.083984375 to 0.083984375
Outputs:
- advanced_walkers: float32 [256, 64, 512], P(('walk', 'pair'))
- log_importance: float32 [256], P(('walk', 'pair'))
The draws below stay inside these ranges and needn't reach their ends.
All inputs are finite; a program needn't handle non-finite values.
Results may differ from the reference program's by a relative error of at most 0.011.
Values may be sent and summed in bfloat16 or wider, within the bound.
A program may use at most 128 MiB of HBM per device.

```python
import jax
import jax.numpy as jnp
from jax import lax

ORB = 512
OCC = 64
VECS = 4096
WALKERS = 256


def block_levels(key, dims, split, least, high):
    def one(position, blocks):
        heights = jax.random.uniform(jax.random.fold_in(jax.random.fold_in(key, 6), position), (blocks,), jnp.float32, least / len(split), high / len(split))
        return jnp.repeat(jnp.exp(heights), dims[position] // blocks).reshape((-1,) + (1,) * (len(dims) - position - 1))

    level = one(*split[0])
    for cut in split[1:]:
        level = level * one(*cut)
    return level


def bell_draw(rng, dims, deviation, most, cuts=(), kind=jnp.bfloat16):
    factor_of = block_levels(rng, dims, cuts, -0.22, 0.18) if cuts else 1.0
    array = jax.random.normal(rng, dims, jnp.float32) * deviation * factor_of
    return jnp.minimum(jnp.maximum(array, -most), most).astype(kind)


def setup_inputs(seed: int = 0) -> dict:
    arg_keys = jax.random.split(jax.random.key(seed), 6)
    return {
        "walkers": bell_draw(arg_keys[0], (WALKERS, OCC, ORB), 1.0, 6.0, ((0, 128),), jnp.float32),
        "inverse_intersection": bell_draw(arg_keys[1], (WALKERS, OCC, OCC), OCC ** -0.5, 0.75, ((0, 128),), jnp.float32),
        "trial": bell_draw(arg_keys[2], (OCC, ORB), 0.016, 0.095703125, ((1, 8),)),
        "fields": bell_draw(arg_keys[3], (WALKERS, VECS), 1.0, 6.0, ((0, 128),), jnp.float32),
        "cholesky": bell_draw(arg_keys[4], (ORB, ORB, VECS), (0.9 / VECS ** 0.5), 0.083984375, ((0, 16), (1, 8))),
    }


time_root = 0.1


def rounded(values):
    return lax.optimization_barrier(values.astype(jnp.bfloat16)).astype(jnp.float32)


def reference(walkers, inverse_intersection, trial, fields, cholesky):
    highest = lax.Precision.HIGHEST
    rotated = jnp.einsum("wji,wjp->wip", inverse_intersection, walkers, precision=highest)
    rotated = rounded(rotated)
    flat_slab = cholesky.reshape(ORB * ORB, VECS)
    trial_wide = trial.astype(jnp.float32)
    groups = WALKERS // 8

    def bias_block(rotated_block):
        greens = jnp.einsum("wip,iq->wpq", rotated_block, trial_wide, precision=highest)
        greens = greens.astype(jnp.bfloat16).reshape(8, ORB * ORB)
        return jnp.dot(greens, flat_slab, preferred_element_type=jnp.float32)

    force_bias = lax.map(bias_block, rotated.reshape(groups, 8, OCC, ORB)).reshape(WALKERS, VECS)
    bias_shift = -time_root * force_bias
    log_importance = jnp.sum(fields * bias_shift - 0.5 * bias_shift * bias_shift, axis=1)
    shifted = (fields - bias_shift).astype(jnp.bfloat16)

    def propagate(pair_args):
        walker_block, shifted_block = pair_args
        potential = jnp.dot(flat_slab, shifted_block.T, preferred_element_type=jnp.float32)
        potential = rounded(potential).T.reshape(8, ORB, ORB)
        series_term = walker_block
        summed = walker_block
        for degree in range(1, 7):
            series_term = jnp.einsum("kiq,kpq->kip", rounded(series_term), potential, precision=highest) * (-time_root / degree)
            summed = summed + series_term
        return summed

    advanced = lax.map(propagate, (walkers.reshape(groups, 8, OCC, ORB), shifted.reshape(groups, 8, VECS)))
    return advanced.reshape(WALKERS, OCC, ORB), log_importance
```

```python
import functools

import jax
import jax.numpy as jnp
from jax import lax
from jax.experimental import pallas as pl
from jax.experimental.pallas import tpu as pltpu
from jax.sharding import PartitionSpec as P

MESH = pl.DeviceIdType.MESH
F32 = jnp.float32
BF16 = jnp.bfloat16
time_root = 0.1
CHUNKS = 4
FIRST_AXIS = ("x", "y", "z", "x")
REST = {"x": (4, 2, 2), "y": (2, 4, 2), "z": (4, 4)}


def device_of(pos):
    x, y, zh, zl, c = pos
    return (x * 2 + zl, (y * 2 + zh) * 2 + c)


def moved(pos, axis, d):
    x, y, zh, zl, c = pos
    if axis == "x":
        return (lax.rem(x + d, 4), y, zh, zl, c)
    if axis == "y":
        return (x, lax.rem(y + d, 4), zh, zl, c)
    z = lax.rem(zh * 2 + zl + d, 4)
    return (x, y, z // 2, lax.rem(z, 2), c)


def slab_index(axis, pos):
    x, y, zh, zl, _ = pos
    every = slice(None)
    return {"x": (every, every, x), "y": (y,), "z": (every, zh, every, zl)}[axis]


def tile_index(axis, pos):
    x, y, zh, zl, _ = pos
    return {"x": (y, zh, zl), "y": (zh, x, zl), "z": (y, x)}[axis]


def kernel(
    walkers, inverse, trial, fields, cholesky, out, log_out,
    slab, half, diag, send_a, recv_a, wide, left, fields_out, fields_in,
    parts, from_core, sums, shifted, total, send_d, recv_d, potential, logs, logs_in,
    *rest,
):
    first_in = rest[:CHUNKS]
    first_sum = rest[CHUNKS : 2 * CHUNKS]
    slab_sem, send_sem, recv_sem, hop_send, hop_recv = rest[2 * CHUNKS :]
    a, b = lax.axis_index("walk"), lax.axis_index("pair")
    x, zl = a // 2, lax.rem(a, 2)
    c = lax.rem(b, 2)
    y, zh = b // 4, lax.rem(b // 2, 2)
    here = (x, y, zh, zl, c)
    slot = c * 64 + (b // 2) * 8 + a

    def other(i):
        dx, dy, dz, dc = lax.rem(i // 2, 4), lax.rem(i // 8, 4), i // 32, lax.rem(i, 2)
        px, py, pzh, pzl, _ = moved(moved(moved(here, "x", dx), "y", dy), "z", dz)
        return (px, py, pzh, pzl, lax.rem(c + dc, 2))

    def send(src, dst, sems, pos):
        pltpu.make_async_remote_copy(
            src_ref=src, dst_ref=dst, send_sem=sems[0], recv_sem=sems[1],
            device_id=device_of(pos), device_id_type=MESH,
        ).start()

    def wait(ref, sem):
        pltpu.make_async_copy(ref, ref, sem).wait()

    for r in range(32):
        place = (r % 16) * 2 + r // 16
        pltpu.make_async_copy(
            cholesky.at[r], slab.at[pl.ds(place * 64, 64)], slab_sem.at[place // 4]
        ).start()

    barrier = pltpu.get_barrier_semaphore()

    def greet(i, carry):
        pl.semaphore_signal(barrier, inc=1, device_id=device_of(other(i)), device_id_type=MESH)
        return carry

    lax.fori_loop(1, 128, greet, 0)

    for k in range(2):
        turned = jnp.transpose(walkers[k])
        rotated = jnp.dot(
            turned, inverse[k], precision=lax.Precision.HIGHEST, preferred_element_type=F32
        )
        rotated = rotated.reshape(16, 2, 16, 64)
        send_a[:, k] = jnp.concatenate([rotated[:, 0], rotated[:, 1]], axis=-1).astype(BF16)
        for n in range(CHUNKS):
            for to in range(8):
                row = fields[pl.ds(k, 1), pl.ds((n * 8 + to) * 128, 128)]
                fields_out[to, pl.ds(k * 4 + n, 1), :] = row

    pl.semaphore_wait(barrier, 127)

    def send_rotated(i, carry):
        pos = other(i)
        to = device_of(pos)
        send(send_a.at[to[1]], recv_a.at[slot], (send_sem.at[0], recv_sem.at[0]), pos)
        return carry

    lax.fori_loop(1, 128, send_rotated, 0)
    recv_a[slot] = send_a[b]

    def walk_peer(i):
        return (lax.rem(x + i // 2, 4), y, zh, lax.rem(zl + i, 2), c)

    def send_fields(i, carry):
        pos = walk_peer(i)
        to = device_of(pos)
        send(
            fields_out.at[to[0]], fields_in.at[pl.ds(pl.multiple_of(a * 8, 8), 8)],
            (send_sem.at[1], recv_sem.at[1]), pos,
        )
        return carry

    lax.fori_loop(1, 8, send_fields, 0)
    fields_in[pl.ds(pl.multiple_of(a * 8, 8), 8)] = fields_out[a]

    square = jnp.concatenate([trial[...].astype(F32)] * 4, axis=0)
    square = jnp.concatenate([square] * 4, axis=1)
    rows = lax.broadcasted_iota(jnp.int32, (256, 256), 0) // 64
    cols = lax.broadcasted_iota(jnp.int32, (256, 256), 1) // 64
    diag[...] = jnp.where(rows == cols, square, 0.0).astype(BF16)

    def rotate_group(g, carry):
        block = pl.ds(pl.multiple_of(g * 256, 256), 256)
        wait(slab.at[block], slab_sem.at[g])

        def columns(t, carry):
            lanes = pl.ds(pl.multiple_of(t * 256, 256), 256)
            half[block, lanes] = jnp.dot(
                diag[...], slab[block, lanes], preferred_element_type=F32
            ).astype(BF16)
            return carry

        return lax.fori_loop(0, 16, columns, carry)

    lax.fori_loop(0, 8, rotate_group, 0)

    wait(recv_a.at[pl.ds(0, 127)], recv_sem.at[0])

    def regroup(g, carry):
        base = pl.multiple_of(g * 256, 256)
        wide[pl.ds(base, 256), :] = recv_a[pl.ds(g * 8, 8)].astype(F32).reshape(256, 128)
        for j in range(16):
            left[pl.ds(pl.multiple_of(g * 16, 16), 16), pl.ds(j * 128, 128)] = wide[
                pl.ds(base + j, 16, stride=16), :
            ].astype(BF16)
        return carry

    lax.fori_loop(0, 16, regroup, 0)

    def hop(n, stage):
        return hop_send.at[n * 6 + stage], hop_recv.at[n * 6 + stage]

    def bias_chunk(n):
        def columns(t, carry):
            lanes = pl.ds(pl.multiple_of(n * 1024 + t * 256, 256), 256)
            got = jnp.dot(left[...], half[:, lanes], preferred_element_type=F32).astype(BF16)
            for group in range(16):
                for lane in range(2):
                    parts[n, group // 8, (group // 2) % 4, group % 2, t, lane] = got[
                        group * 16 : group * 16 + 16, lane * 128 : lane * 128 + 128
                    ]
            return carry

        lax.fori_loop(0, 4, columns, 0)
        send(parts.at[n, 1 - c], from_core.at[n], hop(n, 0), (x, y, zh, zl, 1 - c))

    def add_core(n):
        wait(from_core.at[n], hop_recv.at[n * 6])

        def add(i, carry):
            both = parts[n, c, i].astype(F32) + from_core[n, i].astype(F32)
            parts[n, c, i] = both.astype(BF16)
            return carry

        lax.fori_loop(0, 4, add, 0)
        axis = FIRST_AXIS[n]
        for d in range(1, 4):
            pos = moved(here, axis, d)
            src = parts.at[(n, c) + slab_index(axis, pos)]
            send(src, first_in[n].at[d - 1], hop(n, 1), pos)

    def plane_peer(axis, i):
        one, two = {"x": ("y", "z"), "y": ("z", "x"), "z": ("x", "y")}[axis]
        return moved(moved(here, one, i // 4), two, lax.rem(i, 4))

    def add_first(n):
        axis = FIRST_AXIS[n]
        wait(first_in[n], hop_recv.at[n * 6 + 1])
        got = parts[(n, c) + slab_index(axis, here)].astype(F32)
        for d in range(3):
            got = got + first_in[n][d].astype(F32)
        first_sum[n][...] = got.astype(BF16)

        def give(i, carry):
            pos = plane_peer(axis, i)
            send(first_sum[n].at[tile_index(axis, pos)], sums.at[n, i - 1], hop(n, 2), pos)
            return carry

        lax.fori_loop(1, 16, give, 0)

    def shift(n):
        axis = FIRST_AXIS[n]
        if n == 0:
            wait(fields_in.at[pl.ds(0, 56)], recv_sem.at[1])
        wait(sums.at[n], hop_recv.at[n * 6 + 2])
        bias = first_sum[n][tile_index(axis, here)].astype(F32)
        for i in range(15):
            bias = bias + sums[n, i].astype(F32)
        bias_shift = -time_root * bias
        field = fields_in[pl.ds(n, 16, stride=4), :]
        term = field * bias_shift - 0.5 * bias_shift * bias_shift
        logs[...] = term if n == 0 else logs[...] + term
        place = (n, c, y, zh, x, zl)
        shifted[place] = (field - bias_shift).astype(BF16)

        def give(i, carry):
            send(shifted.at[place], shifted.at[place], hop(n, 3), plane_peer(axis, i))
            return carry

        lax.fori_loop(1, 16, give, 0)
        if n == CHUNKS - 1:
            logs_in[a] = logs[...]

            def give_logs(i, carry):
                sems = send_sem.at[2], recv_sem.at[2]
                send(logs, logs_in.at[a], sems, walk_peer(i))
                return carry

            lax.fori_loop(1, 8, give_logs, 0)

    def spread_plane(n):
        axis = FIRST_AXIS[n]
        wait(sums.at[n], hop_recv.at[n * 6 + 3])
        part = shifted.at[(n, c) + slab_index(axis, here)]
        for d in range(1, 4):
            send(part, part, hop(n, 4), moved(here, axis, d))

    def spread_core(n):
        wait(first_in[n], hop_recv.at[n * 6 + 4])
        part = shifted.at[n, c]
        send(part, part, hop(n, 5), (x, y, zh, zl, 1 - c))

    def potential_chunk(n):
        wait(shifted.at[n, 1 - c], hop_recv.at[n * 6 + 5])

        def columns(t, carry):
            block = pl.ds(pl.multiple_of(t * 256, 256), 256)
            got = jnp.zeros((256, 256), F32) if n == 0 else total[t]
            for i in range(4):
                both = [shifted[n, :, :, :, i, lane].reshape(256, 128) for lane in range(2)]
                got = got + lax.dot_general(
                    jnp.concatenate(both, axis=1),
                    slab[block, pl.ds(n * 1024 + i * 256, 256)],
                    (((1,), (1,)), ((), ())), preferred_element_type=F32,
                )
            if n < CHUNKS - 1:
                total[t] = got
            else:
                for lane in range(2):
                    wide[pl.ds(t * 2 + lane, 256, stride=16), :] = got[
                        :, lane * 128 : lane * 128 + 128
                    ]
            return carry

        lax.fori_loop(0, 8, columns, 0)

    steps = (bias_chunk, add_core, add_first, shift, spread_plane, spread_core, potential_chunk)
    for time in range(len(steps) + CHUNKS - 1):
        for n in range(CHUNKS):
            if 0 <= time - n < len(steps):
                steps[time - n](n)

    def narrow(g, carry):
        block = wide[pl.ds(pl.multiple_of(g * 256, 256), 256), :]
        send_d[pl.ds(g * 8, 8)] = block.astype(BF16).reshape(8, 2, 16, 128)
        return carry

    lax.fori_loop(0, 16, narrow, 0)

    def send_potential(i, carry):
        pos = other(i)
        px, py, pzh, pzl, pc = pos
        to = pc * 64 + (py * 2 + pzh) * 8 + px * 2 + pzl
        send(send_d.at[to], recv_d.at[b, a], (send_sem.at[3], recv_sem.at[3]), pos)
        return carry

    lax.fori_loop(1, 128, send_potential, 0)
    recv_d[b, a] = send_d[slot]

    wait(logs_in.at[pl.ds(0, 7)], recv_sem.at[2])
    all_logs = logs_in[0]
    for i in range(1, 8):
        all_logs = all_logs + logs_in[i]
    log_rows = lax.broadcasted_iota(jnp.int32, (16, 128), 0)
    for k in range(2):
        log_out[k] = jnp.sum(jnp.where(log_rows == a * 2 + k, all_logs, 0.0))

    wait(recv_a.at[pl.ds(0, 127)], recv_sem.at[3])

    def assemble(i, carry):
        for k in range(2):
            for h in range(2):
                for pair in range(4):
                    both = [
                        recv_d[i, pair * 2 + e, k].astype(F32)[:, h * 64 : h * 64 + 64]
                        for e in range(2)
                    ]
                    potential[
                        k, pl.ds(pl.multiple_of(i * 32 + h * 16, 16), 16),
                        pl.ds(pair * 128, 128),
                    ] = jnp.concatenate(both, axis=1).astype(BF16)
        return carry

    lax.fori_loop(0, 16, assemble, 0)

    terms = [walkers[k] for k in range(2)]
    results = list(terms)
    for degree in range(1, 7):
        for k in range(2):
            product = lax.dot_general(
                terms[k].astype(BF16), potential[k], (((1,), (1,)), ((), ())),
                preferred_element_type=F32,
            )
            terms[k] = product * (-time_root / degree)
            results[k] = results[k] + terms[k]
    for k in range(2):
        out[k] = results[k]

    wait(recv_a.at[pl.ds(0, 127)], send_sem.at[0])
    wait(fields_in.at[pl.ds(0, 56)], send_sem.at[1])
    wait(logs_in.at[pl.ds(0, 7)], send_sem.at[2])
    wait(recv_a.at[pl.ds(0, 127)], send_sem.at[3])
    for n in range(CHUNKS):
        for stage, size in enumerate(
            (from_core.at[n], first_in[n], sums.at[n], sums.at[n], first_in[n], from_core.at[n])
        ):
            wait(size, hop_send.at[n * 6 + stage])


def per_device(walkers, inverse_intersection, trial, fields, cholesky):
    vmem = pl.BlockSpec(memory_space=pltpu.VMEM)
    tile = (16, 128)
    chunk = (4, 2, 4, 2) + tile
    scratch = [
        pltpu.VMEM((2048, 4096), BF16),
        pltpu.VMEM((2048, 4096), BF16),
        pltpu.VMEM((256, 256), BF16),
        pltpu.VMEM((16, 2) + tile, BF16),
        pltpu.VMEM((128, 2) + tile, BF16),
        pltpu.VMEM((4096, 128), F32),
        pltpu.VMEM((256, 2048), BF16),
        pltpu.VMEM((8, 8, 128), F32),
        pltpu.VMEM((64, 128), F32),
        pltpu.VMEM((CHUNKS, 2) + chunk, BF16),
        pltpu.VMEM((CHUNKS,) + chunk, BF16),
        pltpu.VMEM((CHUNKS, 15) + tile, BF16),
        pltpu.VMEM((CHUNKS, 2) + chunk, BF16),
        pltpu.VMEM((8, 256, 256), F32),
        pltpu.VMEM((128, 2) + tile, BF16),
        pltpu.VMEM((16, 8, 2) + tile, BF16),
        pltpu.VMEM((2, 512, 512), BF16),
        pltpu.VMEM(tile, F32),
        pltpu.VMEM((8,) + tile, F32),
        *[pltpu.VMEM((3,) + REST[axis] + tile, BF16) for axis in FIRST_AXIS],
        *[pltpu.VMEM(REST[axis] + tile, BF16) for axis in FIRST_AXIS],
        pltpu.SemaphoreType.DMA((8,)),
        pltpu.SemaphoreType.DMA((4,)),
        pltpu.SemaphoreType.DMA((4,)),
        pltpu.SemaphoreType.DMA((CHUNKS * 6,)),
        pltpu.SemaphoreType.DMA((CHUNKS * 6,)),
    ]
    advanced, log_importance = pl.pallas_call(
        kernel,
        out_shape=(
            jax.ShapeDtypeStruct(walkers.shape, F32),
            jax.ShapeDtypeStruct((2,), F32),
        ),
        in_specs=[vmem, vmem, vmem, vmem, pl.BlockSpec(memory_space=pl.ANY)],
        out_specs=(vmem, pl.BlockSpec(memory_space=pltpu.SMEM)),
        scratch_shapes=scratch,
        compiler_params=pltpu.CompilerParams(
            collective_id=0, has_side_effects=True, vmem_limit_bytes=62 * 1024 * 1024
        ),
    )(walkers, inverse_intersection, trial, fields, cholesky)
    return advanced, log_importance


def solution(mesh):
    in_specs = (
        P(("walk", "pair"), None, None),
        P(("walk", "pair"), None, None),
        P(None, "walk"),
        P(("walk", "pair"), None),
        P("pair", "walk", None),
    )
    out_specs = (P(("walk", "pair"), None, None), P(("walk", "pair")))
    return jax.shard_map(
        per_device, mesh=mesh, in_specs=in_specs, out_specs=out_specs, check_vma=False
    )
```

```python
import functools

import jax
import jax.numpy as jnp
from jax import lax
from jax.experimental import pallas as pl
from jax.experimental.pallas import tpu as pltpu
from jax.sharding import PartitionSpec as P

MESH = pl.DeviceIdType.MESH
F32 = jnp.float32
BF16 = jnp.bfloat16
time_root = 0.1
CHUNKS = 4
FIRST_AXIS = ("x", "y", "z", "x")
REST = {"x": (4, 2, 2), "y": (2, 4, 2), "z": (4, 4)}


def device_of(pos):
    x, y, zh, zl, c = pos
    return (x * 2 + zl, (y * 2 + zh) * 2 + c)


def moved(pos, axis, d):
    x, y, zh, zl, c = pos
    if axis == "x":
        return (lax.rem(x + d, 4), y, zh, zl, c)
    if axis == "y":
        return (x, lax.rem(y + d, 4), zh, zl, c)
    z = lax.rem(zh * 2 + zl + d, 4)
    return (x, y, z // 2, lax.rem(z, 2), c)


def slab_index(axis, pos):
    x, y, zh, zl, _ = pos
    every = slice(None)
    return {"x": (every, every, x), "y": (y,), "z": (every, zh, every, zl)}[axis]


def tile_index(axis, pos):
    x, y, zh, zl, _ = pos
    return {"x": (y, zh, zl), "y": (zh, x, zl), "z": (y, x)}[axis]


def kernel(
    walkers, inverse, trial, fields, cholesky, out, log_out,
    slab, half, diag, send_a, recv_a, wide, left, fields_out, fields_in,
    parts, from_core, sums, shifted, total, send_d, recv_d, potential, logs, logs_in,
    *rest,
):
    first_in = rest[:CHUNKS]
    first_sum = rest[CHUNKS : 2 * CHUNKS]
    slab_sem, send_sem, recv_sem, hop_send, hop_recv = rest[2 * CHUNKS :]
    a, b = lax.axis_index("walk"), lax.axis_index("pair")
    x, zl = a // 2, lax.rem(a, 2)
    c = lax.rem(b, 2)
    y, zh = b // 4, lax.rem(b // 2, 2)
    here = (x, y, zh, zl, c)
    slot = c * 64 + (b // 2) * 8 + a

    def other(i):
        dx, dy, dz, dc = lax.rem(i // 2, 4), lax.rem(i // 8, 4), i // 32, lax.rem(i, 2)
        px, py, pzh, pzl, _ = moved(moved(moved(here, "x", dx), "y", dy), "z", dz)
        return (px, py, pzh, pzl, lax.rem(c + dc, 2))

    def send(src, dst, sems, pos):
        pltpu.make_async_remote_copy(
            src_ref=src, dst_ref=dst, send_sem=sems[0], recv_sem=sems[1],
            device_id=device_of(pos), device_id_type=MESH,
        ).start()

    def wait(ref, sem):
        pltpu.make_async_copy(ref, ref, sem).wait()

    for r in range(32):
        place = (r % 16) * 2 + r // 16
        pltpu.make_async_copy(
            cholesky.at[r], slab.at[pl.ds(place * 64, 64)], slab_sem.at[place // 4]
        ).start()

    barrier = pltpu.get_barrier_semaphore()

    def greet(i, carry):
        pl.semaphore_signal(barrier, inc=1, device_id=device_of(other(i)), device_id_type=MESH)
        return carry

    lax.fori_loop(1, 128, greet, 0)

    for k in range(2):
        turned = jnp.transpose(walkers[k])
        rotated = jnp.dot(
            turned, inverse[k], precision=lax.Precision.HIGHEST, preferred_element_type=F32
        )
        rotated = rotated.reshape(16, 2, 16, 64)
        send_a[:, k] = jnp.concatenate([rotated[:, 0], rotated[:, 1]], axis=-1).astype(BF16)
        for n in range(CHUNKS):
            for to in range(8):
                row = fields[pl.ds(k, 1), pl.ds((n * 8 + to) * 128, 128)]
                fields_out[to, pl.ds(k * 4 + n, 1), :] = row

    square = jnp.concatenate([trial[...].astype(F32)] * 4, axis=0)
    square = jnp.concatenate([square] * 4, axis=1)
    rows = lax.broadcasted_iota(jnp.int32, (256, 256), 0) // 64
    cols = lax.broadcasted_iota(jnp.int32, (256, 256), 1) // 64
    diag[...] = jnp.where(rows == cols, square, 0.0).astype(BF16)

    def rotate_group(g, carry):
        block = pl.ds(pl.multiple_of(g * 256, 256), 256)
        wait(slab.at[block], slab_sem.at[g])

        half[block] = jnp.dot(diag[...], slab[block], preferred_element_type=F32).astype(BF16)
        return carry

    lax.fori_loop(0, 8, rotate_group, 0)

    pl.semaphore_wait(barrier, 127)

    def send_rotated(i, carry):
        pos = other(i)
        to = device_of(pos)
        send(send_a.at[to[1]], recv_a.at[slot], (send_sem.at[0], recv_sem.at[0]), pos)
        return carry

    lax.fori_loop(1, 128, send_rotated, 0)
    recv_a[slot] = send_a[b]

    def walk_peer(i):
        return (lax.rem(x + i // 2, 4), y, zh, lax.rem(zl + i, 2), c)

    def send_fields(i, carry):
        pos = walk_peer(i)
        to = device_of(pos)
        send(
            fields_out.at[to[0]], fields_in.at[pl.ds(pl.multiple_of(a * 8, 8), 8)],
            (send_sem.at[1], recv_sem.at[1]), pos,
        )
        return carry

    lax.fori_loop(1, 8, send_fields, 0)
    fields_in[pl.ds(pl.multiple_of(a * 8, 8), 8)] = fields_out[a]

    wait(recv_a.at[pl.ds(0, 127)], recv_sem.at[0])

    def regroup(g, carry):
        base = pl.multiple_of(g * 256, 256)
        wide[pl.ds(base, 256), :] = recv_a[pl.ds(g * 8, 8)].astype(F32).reshape(256, 128)
        for j in range(16):
            left[pl.ds(pl.multiple_of(g * 16, 16), 16), pl.ds(j * 128, 128)] = wide[
                pl.ds(base + j, 16, stride=16), :
            ].astype(BF16)
        return carry

    lax.fori_loop(0, 16, regroup, 0)

    def hop(n, stage):
        return hop_send.at[n * 6 + stage], hop_recv.at[n * 6 + stage]

    def bias_chunk(n):
        got = jnp.dot(
            left[...], half[:, pl.ds(n * 1024, 1024)], preferred_element_type=F32
        ).astype(BF16)
        for group in range(16):
            for lane in range(8):
                parts[n, group // 8, (group // 2) % 4, group % 2, lane // 2, lane % 2] = got[
                    group * 16 : group * 16 + 16, lane * 128 : lane * 128 + 128
                ]
        send(parts.at[n, 1 - c], from_core.at[n], hop(n, 0), (x, y, zh, zl, 1 - c))

    def add_core(n):
        wait(from_core.at[n], hop_recv.at[n * 6])

        def add(i, carry):
            both = parts[n, c, i].astype(F32) + from_core[n, i].astype(F32)
            parts[n, c, i] = both.astype(BF16)
            return carry

        lax.fori_loop(0, 4, add, 0)
        axis = FIRST_AXIS[n]
        for d in range(1, 4):
            pos = moved(here, axis, d)
            src = parts.at[(n, c) + slab_index(axis, pos)]
            send(src, first_in[n].at[d - 1], hop(n, 1), pos)

    def plane_peer(axis, i):
        one, two = {"x": ("y", "z"), "y": ("z", "x"), "z": ("x", "y")}[axis]
        return moved(moved(here, one, i // 4), two, lax.rem(i, 4))

    def add_first(n):
        axis = FIRST_AXIS[n]
        wait(first_in[n], hop_recv.at[n * 6 + 1])
        got = parts[(n, c) + slab_index(axis, here)].astype(F32)
        for d in range(3):
            got = got + first_in[n][d].astype(F32)
        first_sum[n][...] = got.astype(BF16)

        def give(i, carry):
            pos = plane_peer(axis, i)
            send(first_sum[n].at[tile_index(axis, pos)], sums.at[n, i - 1], hop(n, 2), pos)
            return carry

        lax.fori_loop(1, 16, give, 0)

    def shift(n):
        axis = FIRST_AXIS[n]
        if n == 0:
            wait(fields_in.at[pl.ds(0, 56)], recv_sem.at[1])
        wait(sums.at[n], hop_recv.at[n * 6 + 2])
        bias = first_sum[n][tile_index(axis, here)].astype(F32)
        for i in range(15):
            bias = bias + sums[n, i].astype(F32)
        bias_shift = -time_root * bias
        field = fields_in[pl.ds(n, 16, stride=4), :]
        term = field * bias_shift - 0.5 * bias_shift * bias_shift
        logs[...] = term if n == 0 else logs[...] + term
        place = (n, c, y, zh, x, zl)
        shifted[place] = (field - bias_shift).astype(BF16)

        def give(i, carry):
            send(shifted.at[place], shifted.at[place], hop(n, 3), plane_peer(axis, i))
            return carry

        lax.fori_loop(1, 16, give, 0)
        if n == CHUNKS - 1:
            logs_in[a] = logs[...]

            def give_logs(i, carry):
                sems = send_sem.at[2], recv_sem.at[2]
                send(logs, logs_in.at[a], sems, walk_peer(i))
                return carry

            lax.fori_loop(1, 8, give_logs, 0)

    def spread_plane(n):
        axis = FIRST_AXIS[n]
        wait(sums.at[n], hop_recv.at[n * 6 + 3])
        part = shifted.at[(n, c) + slab_index(axis, here)]
        for d in range(1, 4):
            send(part, part, hop(n, 4), moved(here, axis, d))

    def spread_core(n):
        wait(first_in[n], hop_recv.at[n * 6 + 4])
        part = shifted.at[n, c]
        send(part, part, hop(n, 5), (x, y, zh, zl, 1 - c))

    def potential_chunk(n):
        wait(shifted.at[n, 1 - c], hop_recv.at[n * 6 + 5])

        def columns(t, carry):
            block = pl.ds(pl.multiple_of(t * 1024, 1024), 1024)
            lanes = [shifted[n, :, :, :, i // 2, i % 2].reshape(256, 128) for i in range(8)]
            got = lax.dot_general(
                jnp.concatenate(lanes, axis=1), slab[block, pl.ds(n * 1024, 1024)],
                (((1,), (1,)), ((), ())), preferred_element_type=F32,
            )
            if n > 0:
                got = got + total[t]
            if n < CHUNKS - 1:
                total[t] = got
            else:
                for lane in range(8):
                    wide[pl.ds(t * 8 + lane, 256, stride=16), :] = got[
                        :, lane * 128 : lane * 128 + 128
                    ]
            return carry

        lax.fori_loop(0, 2, columns, 0)

    steps = (bias_chunk, add_core, add_first, shift, spread_plane, spread_core, potential_chunk)
    for time in range(len(steps) + CHUNKS - 1):
        for n in range(CHUNKS):
            if 0 <= time - n < len(steps):
                steps[time - n](n)

    def narrow(g, carry):
        block = wide[pl.ds(pl.multiple_of(g * 256, 256), 256), :]
        send_d[pl.ds(g * 8, 8)] = block.astype(BF16).reshape(8, 2, 16, 128)
        return carry

    lax.fori_loop(0, 16, narrow, 0)

    def send_potential(i, carry):
        pos = other(i)
        px, py, pzh, pzl, pc = pos
        to = pc * 64 + (py * 2 + pzh) * 8 + px * 2 + pzl
        send(send_d.at[to], recv_d.at[b, a], (send_sem.at[3], recv_sem.at[3]), pos)
        return carry

    lax.fori_loop(1, 128, send_potential, 0)
    recv_d[b, a] = send_d[slot]

    wait(logs_in.at[pl.ds(0, 7)], recv_sem.at[2])
    all_logs = logs_in[0]
    for i in range(1, 8):
        all_logs = all_logs + logs_in[i]
    log_rows = lax.broadcasted_iota(jnp.int32, (16, 128), 0)
    for k in range(2):
        log_out[k] = jnp.sum(jnp.where(log_rows == a * 2 + k, all_logs, 0.0))

    wait(recv_a.at[pl.ds(0, 127)], recv_sem.at[3])

    def assemble(i, carry):
        for k in range(2):
            for h in range(2):
                for pair in range(4):
                    both = [
                        recv_d[i, pair * 2 + e, k].astype(F32)[:, h * 64 : h * 64 + 64]
                        for e in range(2)
                    ]
                    potential[
                        k, pl.ds(pl.multiple_of(i * 32 + h * 16, 16), 16),
                        pl.ds(pair * 128, 128),
                    ] = jnp.concatenate(both, axis=1).astype(BF16)
        return carry

    lax.fori_loop(0, 16, assemble, 0)

    terms = [walkers[k] for k in range(2)]
    results = list(terms)
    for degree in range(1, 7):
        for k in range(2):
            product = lax.dot_general(
                terms[k].astype(BF16), potential[k], (((1,), (1,)), ((), ())),
                preferred_element_type=F32,
            )
            terms[k] = product * (-time_root / degree)
            results[k] = results[k] + terms[k]
    for k in range(2):
        out[k] = results[k]

    wait(recv_a.at[pl.ds(0, 127)], send_sem.at[0])
    wait(fields_in.at[pl.ds(0, 56)], send_sem.at[1])
    wait(logs_in.at[pl.ds(0, 7)], send_sem.at[2])
    wait(recv_a.at[pl.ds(0, 127)], send_sem.at[3])
    for n in range(CHUNKS):
        for stage, size in enumerate(
            (from_core.at[n], first_in[n], sums.at[n], sums.at[n], first_in[n], from_core.at[n])
        ):
            wait(size, hop_send.at[n * 6 + stage])


def per_device(walkers, inverse_intersection, trial, fields, cholesky):
    vmem = pl.BlockSpec(memory_space=pltpu.VMEM)
    tile = (16, 128)
    chunk = (4, 2, 4, 2) + tile
    scratch = [
        pltpu.VMEM((2048, 4096), BF16),
        pltpu.VMEM((2048, 4096), BF16),
        pltpu.VMEM((256, 256), BF16),
        pltpu.VMEM((16, 2) + tile, BF16),
        pltpu.VMEM((128, 2) + tile, BF16),
        pltpu.VMEM((4096, 128), F32),
        pltpu.VMEM((256, 2048), BF16),
        pltpu.VMEM((8, 8, 128), F32),
        pltpu.VMEM((64, 128), F32),
        pltpu.VMEM((CHUNKS, 2) + chunk, BF16),
        pltpu.VMEM((CHUNKS,) + chunk, BF16),
        pltpu.VMEM((CHUNKS, 15) + tile, BF16),
        pltpu.VMEM((CHUNKS, 2) + chunk, BF16),
        pltpu.VMEM((2, 256, 1024), F32),
        pltpu.VMEM((128, 2) + tile, BF16),
        pltpu.VMEM((16, 8, 2) + tile, BF16),
        pltpu.VMEM((2, 512, 512), BF16),
        pltpu.VMEM(tile, F32),
        pltpu.VMEM((8,) + tile, F32),
        *[pltpu.VMEM((3,) + REST[axis] + tile, BF16) for axis in FIRST_AXIS],
        *[pltpu.VMEM(REST[axis] + tile, BF16) for axis in FIRST_AXIS],
        pltpu.SemaphoreType.DMA((8,)),
        pltpu.SemaphoreType.DMA((4,)),
        pltpu.SemaphoreType.DMA((4,)),
        pltpu.SemaphoreType.DMA((CHUNKS * 6,)),
        pltpu.SemaphoreType.DMA((CHUNKS * 6,)),
    ]
    advanced, log_importance = pl.pallas_call(
        kernel,
        out_shape=(
            jax.ShapeDtypeStruct(walkers.shape, F32),
            jax.ShapeDtypeStruct((2,), F32),
        ),
        in_specs=[vmem, vmem, vmem, vmem, pl.BlockSpec(memory_space=pl.ANY)],
        out_specs=(vmem, pl.BlockSpec(memory_space=pltpu.SMEM)),
        scratch_shapes=scratch,
        compiler_params=pltpu.CompilerParams(
            collective_id=0, has_side_effects=True, vmem_limit_bytes=62 * 1024 * 1024
        ),
    )(walkers, inverse_intersection, trial, fields, cholesky)
    return advanced, log_importance


def solution(mesh):
    in_specs = (
        P(("walk", "pair"), None, None),
        P(("walk", "pair"), None, None),
        P(None, "walk"),
        P(("walk", "pair"), None),
        P("pair", "walk", None),
    )
    out_specs = (P(("walk", "pair"), None, None), P(("walk", "pair")))
    return jax.shard_map(
        per_device, mesh=mesh, in_specs=in_specs, out_specs=out_specs, check_vma=False
    )
```

```python
import functools

import jax
import jax.numpy as jnp
from jax import lax
from jax.experimental import pallas as pl
from jax.experimental.pallas import tpu as pltpu
from jax.sharding import PartitionSpec as P

MESH = pl.DeviceIdType.MESH
F32 = jnp.float32
BF16 = jnp.bfloat16
time_root = 0.1
CHUNKS = 4
STAGES = 3
FIRST_AXIS = ("x", "y", "z", "x")
REST = {"x": (4, 2, 2), "y": (2, 4, 2), "z": (4, 4)}


def device_of(pos):
    x, y, zh, zl, c = pos
    return (x * 2 + zl, (y * 2 + zh) * 2 + c)


def moved(pos, axis, d):
    x, y, zh, zl, c = pos
    if axis == "x":
        return (lax.rem(x + d, 4), y, zh, zl, c)
    if axis == "y":
        return (x, lax.rem(y + d, 4), zh, zl, c)
    z = lax.rem(zh * 2 + zl + d, 4)
    return (x, y, z // 2, lax.rem(z, 2), c)


def slab_index(axis, pos):
    x, y, zh, zl, _ = pos
    every = slice(None)
    return {"x": (every, every, x), "y": (y,), "z": (every, zh, every, zl)}[axis]


def tile_index(axis, pos):
    x, y, zh, zl, _ = pos
    return {"x": (y, zh, zl), "y": (zh, x, zl), "z": (y, x)}[axis]


def kernel(
    walkers, inverse, trial, fields, cholesky, out, log_out,
    stage, half, turned, diag, send_a, recv_a, pass_a, wide, left, fields_out, fields_in,
    parts, from_core, sums, shifted, moved_fields, total, send_d, recv_d, pass_d, potential,
    logs, logs_in, *rest,
):
    first_in = rest[:CHUNKS]
    first_sum = rest[CHUNKS : 2 * CHUNKS]
    slab_sem, send_sem, recv_sem, hop_send, hop_recv = rest[2 * CHUNKS :]
    a, b = lax.axis_index("walk"), lax.axis_index("pair")
    x, zl = a // 2, lax.rem(a, 2)
    c = lax.rem(b, 2)
    y, zh = b // 4, lax.rem(b // 2, 2)
    here = (x, y, zh, zl, c)
    sibling = (x, y, zh, zl, 1 - c)

    def chip_of(pos):
        return (pos[1] * 2 + pos[2]) * 8 + pos[0] * 2 + pos[3]

    chip = chip_of(here)

    def other(i):
        i = lax.rem(i * 37, 64)
        pos = moved(here, "x", lax.rem(i, 4))
        return moved(moved(pos, "y", lax.rem(i // 4, 4)), "z", i // 16)

    def walk_peer(i):
        return (lax.rem(x + i // 2, 4), y, zh, lax.rem(zl + i, 2), c)

    def plane_peer(axis, i):
        one, two = {"x": ("y", "z"), "y": ("z", "x"), "z": ("x", "y")}[axis]
        return moved(moved(here, one, i // 4), two, lax.rem(i, 4))

    def send(src, dst, sems, pos):
        pltpu.make_async_remote_copy(
            src_ref=src, dst_ref=dst, send_sem=sems[0], recv_sem=sems[1],
            device_id=device_of(pos), device_id_type=MESH,
        ).start()

    def wait(ref, sem):
        pltpu.make_async_copy(ref, ref, sem).wait()

    def pair_sems(i):
        return send_sem.at[i], recv_sem.at[i]

    def hop(n, step):
        return hop_send.at[n * 6 + step], hop_recv.at[n * 6 + step]

    def load(g):
        for q in range(4):
            pltpu.make_async_copy(
                cholesky.at[(q % 2) * 16 + g * 2 + q // 2],
                stage.at[lax.rem(g, STAGES), pl.ds(q * 64, 64)],
                slab_sem.at[g],
            ).start()

    barrier = pltpu.get_barrier_semaphore()

    def greet(i, carry):
        pl.semaphore_signal(barrier, inc=1, device_id=device_of(other(i)), device_id_type=MESH)
        return carry

    pl.semaphore_signal(barrier, inc=1, device_id=device_of(sibling), device_id_type=MESH)
    lax.fori_loop(1, 64, greet, 0)

    for g in range(STAGES):
        load(jnp.int32(g))

    for k in range(2):
        flipped = jnp.transpose(walkers[k])
        rotated = jnp.dot(
            flipped, inverse[k], precision=lax.Precision.HIGHEST, preferred_element_type=F32
        )
        rotated = rotated.reshape(16, 2, 16, 64)
        rotated = jnp.concatenate([rotated[:, 0], rotated[:, 1]], axis=-1).astype(BF16)
        send_a[k] = rotated.reshape(8, 2, 16, 128)

    pl.semaphore_wait(barrier, 64)

    for k in range(2):

        def send_rotated(i, carry, k=k):
            pos = other(i)
            src = send_a.at[k, pos[1] * 2 + pos[2]]
            send(src, recv_a.at[k, :, chip], pair_sems(k), pos)
            return carry

        lax.fori_loop(1, 64, send_rotated, 0)
        recv_a[k, :, chip] = send_a[k, y * 2 + zh]

    for k in range(2):
        for to in range(8):
            for lane in range(4):
                at = (lane // 2) * 2048 + to * 256 + (lane % 2) * 128
                fields_out[to, pl.ds(k * 4 + lane, 1), :] = fields[pl.ds(k, 1), pl.ds(at, 128)]
    mine = pl.ds(pl.multiple_of(a * 8, 8), 8)

    def send_fields(i, carry):
        pos = walk_peer(i)
        send(fields_out.at[device_of(pos)[0]], fields_in.at[mine], pair_sems(2), pos)
        return carry

    lax.fori_loop(1, 8, send_fields, 0)
    fields_in[mine] = fields_out[a]

    square = jnp.concatenate([trial[...].astype(F32)] * 4, axis=0)
    square = jnp.concatenate([square] * 4, axis=1)
    rows = lax.broadcasted_iota(jnp.int32, (256, 256), 0) // 64
    cols = lax.broadcasted_iota(jnp.int32, (256, 256), 1) // 64
    diag[...] = jnp.where(rows == cols, square, 0.0).astype(BF16)

    for g in range(8):
        block = pl.ds(g * 256, 256)
        wait(stage.at[g % STAGES], slab_sem.at[g])
        half[block] = jnp.dot(
            diag[...], stage[g % STAGES], preferred_element_type=F32
        ).astype(BF16)
        turned[:, block] = jnp.transpose(stage[g % STAGES])
        if g + STAGES < 8:
            load(jnp.int32(g + STAGES))

    def regroup(k, side, source):
        def some(g, carry):
            base = pl.multiple_of(side * 1024 + g * 256, 256)
            wide[pl.ds(base, 256), :] = source[pl.ds(g * 16, 16)].astype(F32).reshape(256, 128)
            for j in range(16):
                left[
                    k, pl.ds(pl.multiple_of(side * 64 + g * 16, 16), 16), pl.ds(j * 128, 128)
                ] = wide[pl.ds(base + j, 16, stride=16), :].astype(BF16)
            return carry

        lax.fori_loop(0, 4, some, 0)

    def receive(k):
        wait(recv_a.at[k, :, pl.ds(0, 63)], recv_sem.at[k])
        send(recv_a.at[k, 1 - c], pass_a.at[k], pair_sems(3 + k), sibling)
        regroup(k, 0, recv_a.at[k, c])
        wait(pass_a.at[k], recv_sem.at[3 + k])
        regroup(k, 1, pass_a.at[k])

    def bias_chunk(n):
        got = jnp.dot(
            left[n // 2], half[:, pl.ds((n % 2) * 2048, 2048)], preferred_element_type=F32
        )
        for group in range(16):
            for to in range(8):
                tile = [
                    got[group * 8 : group * 8 + 8, at * 128 : at * 128 + 128]
                    for at in (to * 2, to * 2 + 1)
                ]
                parts[n, group // 8, (group // 2) % 4, group % 2, to // 2, to % 2] = (
                    jnp.concatenate(tile, axis=0).astype(BF16)
                )
        send(parts.at[n, 1], from_core.at[n], hop(n, 0), sibling)

    def add_core(n):
        wait(from_core.at[n], hop_recv.at[n * 6])

        def add(i, carry):
            both = parts[n, 0, i].astype(F32) + from_core[n, i].astype(F32)
            parts[n, 0, i] = both.astype(BF16)
            return carry

        lax.fori_loop(0, 4, add, 0)
        axis = FIRST_AXIS[n]
        for d in (2, 1, 3):
            pos = moved(here, axis, d)
            src = parts.at[(n, 0) + slab_index(axis, pos)]
            send(src, first_in[n].at[d - 1], hop(n, 1), pos)

    def add_first(n):
        axis = FIRST_AXIS[n]
        wait(first_in[n], hop_recv.at[n * 6 + 1])
        got = parts[(n, 0) + slab_index(axis, here)].astype(F32)
        for d in range(3):
            got = got + first_in[n][d].astype(F32)
        first_sum[n][...] = got.astype(BF16)

        def give(i, carry):
            pos = plane_peer(axis, i)
            send(first_sum[n].at[tile_index(axis, pos)], sums.at[n, i - 1], hop(n, 2), pos)
            return carry

        lax.fori_loop(1, 16, give, 0)

    def shift(n):
        axis = FIRST_AXIS[n]
        if n == 0:
            wait(fields_in.at[pl.ds(0, 56)], recv_sem.at[2])
        wait(sums.at[n], hop_recv.at[n * 6 + 2])
        bias = first_sum[n][tile_index(axis, here)].astype(F32)
        for i in range(15):
            bias = bias + sums[n, i].astype(F32)
        bias_shift = -time_root * bias
        field = jnp.concatenate(
            [fields_in[pl.ds(n * 2 + lane, 8, stride=8), :] for lane in range(2)], axis=0
        )
        place = (n, 0, y, zh, x, zl)
        shifted[place] = (field - bias_shift).astype(BF16)

        def give(i, carry):
            send(shifted.at[place], shifted.at[place], hop(n, 3), plane_peer(axis, i))
            return carry

        lax.fori_loop(1, 16, give, 0)
        term = field * bias_shift - 0.5 * bias_shift * bias_shift
        term = term[:8] + term[8:]
        rows = pl.ds((n // 2) * 8, 8)
        logs[rows] = term if n % 2 == 0 else logs[rows] + term
        if n == CHUNKS - 1:
            logs_in[a] = logs[...]

            def give_logs(i, carry):
                send(logs, logs_in.at[a], pair_sems(5), walk_peer(i))
                return carry

            lax.fori_loop(1, 8, give_logs, 0)

    def spread_plane(n):
        axis = FIRST_AXIS[n]
        wait(sums.at[n], hop_recv.at[n * 6 + 3])
        part = shifted.at[(n, 0) + slab_index(axis, here)]
        for d in (2, 1, 3):
            send(part, part, hop(n, 4), moved(here, axis, d))

    def spread_core(n):
        wait(first_in[n], hop_recv.at[n * 6 + 4])
        send(shifted.at[n, 0], shifted.at[n, 1], hop(n, 5), sibling)

    def potential_chunk(n):
        wait(shifted.at[n, 1], hop_recv.at[n * 6 + 5])
        for at in range(8):
            tiles = shifted[n, :, :, :, at // 2, at % 2].astype(F32).reshape(16, 16, 128)
            for lane in range(2):
                moved_fields[:, pl.ds((at * 2 + lane) * 128, 128)] = (
                    tiles[:, lane * 8 : lane * 8 + 8].reshape(128, 128).astype(BF16)
                )
        got = jnp.dot(
            moved_fields[...], turned[pl.ds((n % 2) * 2048, 2048)], preferred_element_type=F32
        )
        if n % 2 == 0:
            total[...] = got
        else:
            got = got + total[...]
            for j in range(16):
                wide[pl.ds(j, 128, stride=16), :] = got[:, j * 128 : j * 128 + 128]

    def give_potential(k):
        for side in range(2):

            def narrow(g, carry, side=side):
                block = wide[pl.ds(pl.multiple_of(side * 1024 + g * 256, 256), 256), :]
                send_d[k, pl.ds(g * 16, 16), side] = block.astype(BF16).reshape(16, 16, 128)
                return carry

            lax.fori_loop(0, 4, narrow, 0)

        def give(i, carry):
            pos = other(i)
            send(send_d.at[k, chip_of(pos)], recv_d.at[k, :, chip], pair_sems(6 + k), pos)
            return carry

        lax.fori_loop(1, 64, give, 0)
        recv_d[k, :, chip] = send_d[k, chip]

    def pass_potential(k):
        wait(recv_d.at[k, :, pl.ds(0, 63)], recv_sem.at[6 + k])
        send(recv_d.at[k, 1], pass_d.at[k], pair_sems(8 + k), sibling)

    def assemble(k, core, source):
        def some(i, carry):
            for h in range(2):
                row = pl.multiple_of((i * 2 + core) * 32 + h * 16, 16)
                for pair in range(4):
                    both = [
                        source[i * 8 + pair * 2 + e].astype(F32)[:, h * 64 : h * 64 + 64]
                        for e in range(2)
                    ]
                    potential[k, pl.ds(row, 16), pl.ds(pair * 128, 128)] = jnp.concatenate(
                        both, axis=1
                    ).astype(BF16)
            return carry

        lax.fori_loop(0, 8, some, 0)

    def propagate(k):
        assemble(k, c, recv_d.at[k, 0])
        wait(pass_d.at[k], recv_sem.at[8 + k])
        assemble(k, 1 - c, pass_d.at[k])
        series_term = walkers[k]
        summed = series_term
        for degree in range(1, 7):
            product = lax.dot_general(
                series_term.astype(BF16), potential[k], (((1,), (1,)), ((), ())),
                preferred_element_type=F32,
            )
            series_term = product * (-time_root / degree)
            summed = summed + series_term
        out[k] = summed

    receive(0)
    bias_chunk(0)
    bias_chunk(1)
    add_core(0)
    add_core(1)
    receive(1)
    bias_chunk(2)
    bias_chunk(3)
    add_first(0)
    add_first(1)
    add_core(2)
    add_core(3)
    shift(0)
    shift(1)
    add_first(2)
    add_first(3)
    spread_plane(0)
    spread_plane(1)
    shift(2)
    shift(3)
    spread_core(0)
    spread_core(1)
    spread_plane(2)
    spread_plane(3)
    potential_chunk(0)
    potential_chunk(1)
    give_potential(0)
    spread_core(2)
    spread_core(3)
    potential_chunk(2)
    potential_chunk(3)
    give_potential(1)
    pass_potential(0)
    propagate(0)

    wait(logs_in.at[pl.ds(0, 7)], recv_sem.at[5])
    all_logs = logs_in[0]
    for i in range(1, 8):
        all_logs = all_logs + logs_in[i]
    log_rows = lax.broadcasted_iota(jnp.int32, (16, 128), 0)
    for k in range(2):
        log_out[k] = jnp.sum(jnp.where(log_rows == k * 8 + a, all_logs, 0.0))

    pass_potential(1)
    propagate(1)

    for k in range(2):
        wait(recv_a.at[k, :, pl.ds(0, 63)], send_sem.at[k])
        wait(recv_d.at[k, :, pl.ds(0, 63)], send_sem.at[6 + k])
        wait(pass_a.at[k], send_sem.at[3 + k])
        wait(pass_d.at[k], send_sem.at[8 + k])
    wait(fields_in.at[pl.ds(0, 56)], send_sem.at[2])
    wait(logs_in.at[pl.ds(0, 7)], send_sem.at[5])
    for n in range(CHUNKS):
        for step, size in enumerate(
            (from_core.at[n], first_in[n], sums.at[n], sums.at[n], first_in[n], from_core.at[n])
        ):
            wait(size, hop_send.at[n * 6 + step])


def per_device(walkers, inverse_intersection, trial, fields, cholesky):
    vmem = pl.BlockSpec(memory_space=pltpu.VMEM)
    tile = (16, 128)
    chunk = (4, 2, 4, 2) + tile
    scratch = [
        pltpu.VMEM((STAGES, 256, 4096), BF16),
        pltpu.VMEM((2048, 4096), BF16),
        pltpu.VMEM((4096, 2048), BF16),
        pltpu.VMEM((256, 256), BF16),
        pltpu.VMEM((2, 8, 2) + tile, BF16),
        pltpu.VMEM((2, 2, 64) + tile, BF16),
        pltpu.VMEM((2, 64) + tile, BF16),
        pltpu.VMEM((2048, 128), F32),
        pltpu.VMEM((2, 128, 2048), BF16),
        pltpu.VMEM((8, 8, 128), F32),
        pltpu.VMEM((64, 128), F32),
        pltpu.VMEM((CHUNKS, 2) + chunk, BF16),
        pltpu.VMEM((CHUNKS,) + chunk, BF16),
        pltpu.VMEM((CHUNKS, 15) + tile, BF16),
        pltpu.VMEM((CHUNKS, 2) + chunk, BF16),
        pltpu.VMEM((128, 2048), BF16),
        pltpu.VMEM((128, 2048), F32),
        pltpu.VMEM((2, 64, 2) + tile, BF16),
        pltpu.VMEM((2, 2, 64) + tile, BF16),
        pltpu.VMEM((2, 64) + tile, BF16),
        pltpu.VMEM((2, 512, 512), BF16),
        pltpu.VMEM(tile, F32),
        pltpu.VMEM((8,) + tile, F32),
        *[pltpu.VMEM((3,) + REST[axis] + tile, BF16) for axis in FIRST_AXIS],
        *[pltpu.VMEM(REST[axis] + tile, BF16) for axis in FIRST_AXIS],
        pltpu.SemaphoreType.DMA((8,)),
        pltpu.SemaphoreType.DMA((10,)),
        pltpu.SemaphoreType.DMA((10,)),
        pltpu.SemaphoreType.DMA((CHUNKS * 6,)),
        pltpu.SemaphoreType.DMA((CHUNKS * 6,)),
    ]
    advanced, log_importance = pl.pallas_call(
        kernel,
        out_shape=(
            jax.ShapeDtypeStruct(walkers.shape, F32),
            jax.ShapeDtypeStruct((2,), F32),
        ),
        in_specs=[vmem, vmem, vmem, vmem, pl.BlockSpec(memory_space=pl.ANY)],
        out_specs=(vmem, pl.BlockSpec(memory_space=pltpu.SMEM)),
        scratch_shapes=scratch,
        compiler_params=pltpu.CompilerParams(
            collective_id=0, has_side_effects=True, vmem_limit_bytes=62 * 1024 * 1024
        ),
    )(walkers, inverse_intersection, trial, fields, cholesky)
    return advanced, log_importance


def solution(mesh):
    in_specs = (
        P(("walk", "pair"), None, None),
        P(("walk", "pair"), None, None),
        P(None, "walk"),
        P(("walk", "pair"), None),
        P("pair", "walk", None),
    )
    out_specs = (P(("walk", "pair"), None, None), P(("walk", "pair")))
    return jax.shard_map(
        per_device, mesh=mesh, in_specs=in_specs, out_specs=out_specs, check_vma=False
    )
```

```python
import functools

import jax
import jax.numpy as jnp
from jax import lax
from jax.experimental import pallas as pl
from jax.experimental.pallas import tpu as pltpu
from jax.sharding import PartitionSpec as P

MESH = pl.DeviceIdType.MESH
F32 = jnp.float32
BF16 = jnp.bfloat16
time_root = 0.1
CHUNKS = 4
STAGES = 3
FARTHEST = sorted(range(1, 16), key=lambda i: -min(i // 4, 4 - i // 4) - min(i % 4, 4 - i % 4))
FIRST_AXIS = ("x", "y", "z", "x")
REST = {"x": (4, 2, 2), "y": (2, 4, 2), "z": (4, 4)}


def device_of(pos):
    x, y, zh, zl, c = pos
    return (x * 2 + zl, (y * 2 + zh) * 2 + c)


def moved(pos, axis, d):
    x, y, zh, zl, c = pos
    if axis == "x":
        return (lax.rem(x + d, 4), y, zh, zl, c)
    if axis == "y":
        return (x, lax.rem(y + d, 4), zh, zl, c)
    z = lax.rem(zh * 2 + zl + d, 4)
    return (x, y, z // 2, lax.rem(z, 2), c)


def slab_index(axis, pos):
    x, y, zh, zl, _ = pos
    every = slice(None)
    return {"x": (every, every, x), "y": (y,), "z": (every, zh, every, zl)}[axis]


def tile_index(axis, pos):
    x, y, zh, zl, _ = pos
    return {"x": (y, zh, zl), "y": (zh, x, zl), "z": (y, x)}[axis]


def kernel(
    walkers_in, inverse_in, trial, fields, cholesky, out, log_out,
    walkers, inverse, stage, half, turned, diag, send_a, recv_a, pass_a, wide, left, fields_out, fields_in,
    parts, from_core, sums, shifted, moved_fields, total, send_d, recv_d, pass_d, potential,
    logs, logs_in, *rest,
):
    first_in = rest[:CHUNKS]
    first_sum = rest[CHUNKS : 2 * CHUNKS]
    in_sem, slab_sem, send_sem, recv_sem, hop_send, hop_recv = rest[2 * CHUNKS :]
    a, b = lax.axis_index("walk"), lax.axis_index("pair")
    x, zl = a // 2, lax.rem(a, 2)
    c = lax.rem(b, 2)
    y, zh = b // 4, lax.rem(b // 2, 2)
    here = (x, y, zh, zl, c)
    sibling = (x, y, zh, zl, 1 - c)

    def chip_of(pos):
        return (pos[1] * 2 + pos[2]) * 8 + pos[0] * 2 + pos[3]

    chip = chip_of(here)

    def other(i):
        i = lax.rem(i * 37, 64)
        pos = moved(here, "x", lax.rem(i, 4))
        return moved(moved(pos, "y", lax.rem(i // 4, 4)), "z", i // 16)

    xs = [lax.rem(x + d, 4) for d in range(4)]
    ys = [lax.rem(y + d, 4) for d in range(4)]
    zs = [lax.rem(zh * 2 + zl + d, 4) for d in range(4)]
    far = [
        (xs[i % 4], ys[i // 4 % 4], zs[i // 16] // 2, lax.rem(zs[i // 16], 2), c)
        for i in range(64)
    ]

    def walk_peer(i):
        return (lax.rem(x + i // 2, 4), y, zh, lax.rem(zl + i, 2), c)

    def plane_peer(axis, i):
        one, two = i // 4, i % 4
        dx, dy, dz = {"x": (0, one, two), "y": (two, 0, one), "z": (one, two, 0)}[axis]
        return far[dx + dy * 4 + dz * 16]

    def send(src, dst, sems, pos):
        pltpu.make_async_remote_copy(
            src_ref=src, dst_ref=dst, send_sem=sems[0], recv_sem=sems[1],
            device_id=device_of(pos), device_id_type=MESH,
        ).start()

    def wait(ref, sem):
        pltpu.make_async_copy(ref, ref, sem).wait()

    def pair_sems(i):
        return send_sem.at[i], recv_sem.at[i]

    def hop(n, step):
        return hop_send.at[n * 6 + step], hop_recv.at[n * 6 + step]

    def load(g):
        for q in range(4):
            pltpu.make_async_copy(
                cholesky.at[(q % 2) * 16 + g * 2 + q // 2],
                stage.at[lax.rem(g, STAGES), pl.ds(q * 64, 64)],
                slab_sem.at[g],
            ).start()

    barrier = pltpu.get_barrier_semaphore()
    pl.semaphore_signal(barrier, inc=1, device_id=device_of(sibling), device_id_type=MESH)
    pltpu.make_async_copy(walkers_in, walkers, in_sem.at[0]).start()
    pltpu.make_async_copy(inverse_in, inverse, in_sem.at[1]).start()
    for i in range(1, 64):
        pl.semaphore_signal(
            barrier, inc=1, device_id=device_of(far[i * 37 % 64]), device_id_type=MESH
        )

    def rotate(k):
        flipped = jnp.transpose(walkers[k])
        rotated = jnp.dot(
            flipped, inverse[k], precision=lax.Precision.HIGHEST, preferred_element_type=F32
        )
        rotated = rotated.reshape(16, 2, 16, 64)
        rotated = jnp.concatenate([rotated[:, 0], rotated[:, 1]], axis=-1).astype(BF16)
        send_a[k] = rotated.reshape(8, 2, 16, 128)

    def give_rotated(k):
        def give(i, carry):
            pos = other(i)
            src = send_a.at[k, pos[1] * 2 + pos[2]]
            send(src, recv_a.at[k, :, chip], pair_sems(k), pos)
            return carry

        lax.fori_loop(1, 64, give, 0)
        recv_a[k, :, chip] = send_a[k, y * 2 + zh]

    for g in range(STAGES):
        load(jnp.int32(g))
    wait(walkers, in_sem.at[0])
    wait(inverse, in_sem.at[1])
    rotate(0)
    pl.semaphore_wait(barrier, 64)
    give_rotated(0)
    rotate(1)
    give_rotated(1)

    for k in range(2):
        for to in range(8):
            for lane in range(4):
                at = (lane // 2) * 2048 + to * 256 + (lane % 2) * 128
                fields_out[to, pl.ds(k * 4 + lane, 1), :] = fields[pl.ds(k, 1), pl.ds(at, 128)]
    mine = pl.ds(pl.multiple_of(a * 8, 8), 8)

    def send_fields(i, carry):
        pos = walk_peer(i)
        send(fields_out.at[device_of(pos)[0]], fields_in.at[mine], pair_sems(2), pos)
        return carry

    lax.fori_loop(1, 8, send_fields, 0)
    fields_in[mine] = fields_out[a]

    square = jnp.concatenate([trial[...].astype(F32)] * 4, axis=0)
    square = jnp.concatenate([square] * 4, axis=1)
    rows = lax.broadcasted_iota(jnp.int32, (256, 256), 0) // 64
    cols = lax.broadcasted_iota(jnp.int32, (256, 256), 1) // 64
    diag[...] = jnp.where(rows == cols, square, 0.0).astype(BF16)

    def turn(g, carry):
        block = pl.ds(pl.multiple_of(g * 256, 256), 256)
        now = lax.rem(g, STAGES)
        wait(stage.at[now], slab_sem.at[g])
        half[block] = jnp.dot(diag[...], stage[now], preferred_element_type=F32).astype(BF16)
        turned[:, block] = jnp.transpose(stage[now])

        @pl.when(g + STAGES < 8)
        def _():
            load(g + STAGES)

        return carry

    lax.fori_loop(0, 8, turn, 0)

    def regroup(k, side, source):
        def some(g, carry):
            base = pl.multiple_of(side * 1024 + g * 256, 256)
            wide[pl.ds(base, 256), :] = source[pl.ds(g * 16, 16)].astype(F32).reshape(256, 128)
            for j in range(16):
                left[
                    k, pl.ds(pl.multiple_of(side * 64 + g * 16, 16), 16), pl.ds(j * 128, 128)
                ] = wide[pl.ds(base + j, 16, stride=16), :].astype(BF16)
            return carry

        lax.fori_loop(0, 4, some, 0)

    def receive(k):
        wait(recv_a.at[k, :, pl.ds(0, 63)], recv_sem.at[k])
        send(recv_a.at[k, 1 - c], pass_a.at[k], pair_sems(3 + k), sibling)
        regroup(k, 0, recv_a.at[k, c])
        wait(pass_a.at[k], recv_sem.at[3 + k])
        regroup(k, 1, pass_a.at[k])

    def bias_chunk(n):
        got = jnp.dot(
            left[n // 2], half[:, pl.ds((n % 2) * 2048, 2048)], preferred_element_type=F32
        )
        for group in range(16):
            for to in range(8):
                tile = [
                    got[group * 8 : group * 8 + 8, at * 128 : at * 128 + 128]
                    for at in (to * 2, to * 2 + 1)
                ]
                parts[n, group // 8, (group // 2) % 4, group % 2, to // 2, to % 2] = (
                    jnp.concatenate(tile, axis=0).astype(BF16)
                )
        send(parts.at[n, 1], from_core.at[n], hop(n, 0), sibling)

    def add_core(n):
        wait(from_core.at[n], hop_recv.at[n * 6])

        def add(i, carry):
            both = parts[n, 0, i].astype(F32) + from_core[n, i].astype(F32)
            parts[n, 0, i] = both.astype(BF16)
            return carry

        lax.fori_loop(0, 4, add, 0)
        axis = FIRST_AXIS[n]
        for d in (2, 1, 3):
            pos = moved(here, axis, d)
            src = parts.at[(n, 0) + slab_index(axis, pos)]
            send(src, first_in[n].at[d - 1], hop(n, 1), pos)

    def add_first(n):
        axis = FIRST_AXIS[n]
        wait(first_in[n], hop_recv.at[n * 6 + 1])
        got = parts[(n, 0) + slab_index(axis, here)].astype(F32)
        for d in range(3):
            got = got + first_in[n][d].astype(F32)
        first_sum[n][...] = got.astype(BF16)

        for i in FARTHEST:
            pos = plane_peer(axis, i)
            send(first_sum[n].at[tile_index(axis, pos)], sums.at[n, i - 1], hop(n, 2), pos)

    def shift(n):
        axis = FIRST_AXIS[n]
        if n == 0:
            wait(fields_in.at[pl.ds(0, 56)], recv_sem.at[2])
        wait(sums.at[n], hop_recv.at[n * 6 + 2])
        bias = first_sum[n][tile_index(axis, here)].astype(F32)
        for i in range(15):
            bias = bias + sums[n, i].astype(F32)
        bias_shift = -time_root * bias
        field = jnp.concatenate(
            [fields_in[pl.ds(n * 2 + lane, 8, stride=8), :] for lane in range(2)], axis=0
        )
        place = (n, 0, y, zh, x, zl)
        shifted[place] = (field - bias_shift).astype(BF16)

        for i in FARTHEST:
            send(shifted.at[place], shifted.at[place], hop(n, 3), plane_peer(axis, i))
        term = field * bias_shift - 0.5 * bias_shift * bias_shift
        term = term[:8] + term[8:]
        rows = pl.ds((n // 2) * 8, 8)
        logs[rows] = term if n % 2 == 0 else logs[rows] + term
        if n == CHUNKS - 1:
            logs_in[a] = logs[...]

            def give_logs(i, carry):
                send(logs, logs_in.at[a], pair_sems(5), walk_peer(i))
                return carry

            lax.fori_loop(1, 8, give_logs, 0)

    def spread_plane(n):
        axis = FIRST_AXIS[n]
        wait(sums.at[n], hop_recv.at[n * 6 + 3])
        part = shifted.at[(n, 0) + slab_index(axis, here)]
        for d in (2, 1, 3):
            send(part, part, hop(n, 4), moved(here, axis, d))

    def spread_core(n):
        wait(first_in[n], hop_recv.at[n * 6 + 4])
        send(shifted.at[n, 0], shifted.at[n, 1], hop(n, 5), sibling)

    def potential_chunk(n):
        wait(shifted.at[n, 1], hop_recv.at[n * 6 + 5])
        for at in range(8):
            tiles = shifted[n, :, :, :, at // 2, at % 2].astype(F32).reshape(16, 16, 128)
            for lane in range(2):
                moved_fields[:, pl.ds((at * 2 + lane) * 128, 128)] = (
                    tiles[:, lane * 8 : lane * 8 + 8].reshape(128, 128).astype(BF16)
                )
        got = jnp.dot(
            moved_fields[...], turned[pl.ds((n % 2) * 2048, 2048)], preferred_element_type=F32
        )
        if n % 2 == 0:
            total[...] = got
        else:
            got = got + total[...]
            for j in range(16):
                wide[pl.ds(j, 128, stride=16), :] = got[:, j * 128 : j * 128 + 128]

    def give_potential(k):
        for side in range(2):

            def narrow(g, carry, side=side):
                block = wide[pl.ds(pl.multiple_of(side * 1024 + g * 256, 256), 256), :]
                send_d[k, pl.ds(g * 16, 16), side] = block.astype(BF16).reshape(16, 16, 128)
                return carry

            lax.fori_loop(0, 4, narrow, 0)

        def give(i, carry):
            pos = other(i)
            send(send_d.at[k, chip_of(pos)], recv_d.at[k, :, chip], pair_sems(6 + k), pos)
            return carry

        lax.fori_loop(1, 64, give, 0)
        recv_d[k, :, chip] = send_d[k, chip]

    def pass_potential(k):
        wait(recv_d.at[k, :, pl.ds(0, 63)], recv_sem.at[6 + k])
        send(recv_d.at[k, 1], pass_d.at[k], pair_sems(8 + k), sibling)

    def assemble(k, core, source):
        def some(i, carry):
            for h in range(2):
                row = pl.multiple_of((i * 2 + core) * 32 + h * 16, 16)
                for pair in range(4):
                    both = [
                        source[i * 8 + pair * 2 + e].astype(F32)[:, h * 64 : h * 64 + 64]
                        for e in range(2)
                    ]
                    potential[k, pl.ds(row, 16), pl.ds(pair * 128, 128)] = jnp.concatenate(
                        both, axis=1
                    ).astype(BF16)
            return carry

        lax.fori_loop(0, 8, some, 0)

    def propagate(k):
        assemble(k, c, recv_d.at[k, 0])
        wait(pass_d.at[k], recv_sem.at[8 + k])
        assemble(k, 1 - c, pass_d.at[k])
        series_term = walkers[k]
        summed = series_term
        for degree in range(1, 7):
            product = lax.dot_general(
                series_term.astype(BF16), potential[k], (((1,), (1,)), ((), ())),
                preferred_element_type=F32,
            )
            series_term = product * (-time_root / degree)
            summed = summed + series_term
        out[k] = summed

    receive(0)
    bias_chunk(0)
    bias_chunk(1)
    add_core(0)
    add_core(1)
    receive(1)
    bias_chunk(2)
    bias_chunk(3)
    add_first(0)
    add_first(1)
    add_core(2)
    add_core(3)
    shift(0)
    shift(1)
    add_first(2)
    add_first(3)
    spread_plane(0)
    spread_plane(1)
    shift(2)
    shift(3)
    spread_core(0)
    spread_core(1)
    spread_plane(2)
    spread_plane(3)
    potential_chunk(0)
    potential_chunk(1)
    give_potential(0)
    spread_core(2)
    spread_core(3)
    potential_chunk(2)
    potential_chunk(3)
    give_potential(1)
    pass_potential(0)
    propagate(0)

    wait(logs_in.at[pl.ds(0, 7)], recv_sem.at[5])
    all_logs = logs_in[0]
    for i in range(1, 8):
        all_logs = all_logs + logs_in[i]
    log_rows = lax.broadcasted_iota(jnp.int32, (16, 128), 0)
    for k in range(2):
        log_out[k] = jnp.sum(jnp.where(log_rows == k * 8 + a, all_logs, 0.0))

    pass_potential(1)
    propagate(1)

    for k in range(2):
        wait(recv_a.at[k, :, pl.ds(0, 63)], send_sem.at[k])
        wait(recv_d.at[k, :, pl.ds(0, 63)], send_sem.at[6 + k])
        wait(pass_a.at[k], send_sem.at[3 + k])
        wait(pass_d.at[k], send_sem.at[8 + k])
    wait(fields_in.at[pl.ds(0, 56)], send_sem.at[2])
    wait(logs_in.at[pl.ds(0, 7)], send_sem.at[5])
    for n in range(CHUNKS):
        for step, size in enumerate(
            (from_core.at[n], first_in[n], sums.at[n], sums.at[n], first_in[n], from_core.at[n])
        ):
            wait(size, hop_send.at[n * 6 + step])


def settle(result, log, out, log_out):
    out[...] = result[...]
    for k in range(2):
        log_out[k] = log[k]


def per_device(walkers, inverse_intersection, trial, fields, cholesky):
    vmem = pl.BlockSpec(memory_space=pltpu.VMEM)
    whole = pl.BlockSpec(memory_space=pl.ANY)
    tile = (16, 128)
    chunk = (4, 2, 4, 2) + tile
    scratch = [
        pltpu.VMEM(walkers.shape, F32),
        pltpu.VMEM(inverse_intersection.shape, F32),
        pltpu.VMEM((STAGES, 256, 4096), BF16),
        pltpu.VMEM((2048, 4096), BF16),
        pltpu.VMEM((4096, 2048), BF16),
        pltpu.VMEM((256, 256), BF16),
        pltpu.VMEM((2, 8, 2) + tile, BF16),
        pltpu.VMEM((2, 2, 64) + tile, BF16),
        pltpu.VMEM((2, 64) + tile, BF16),
        pltpu.VMEM((2048, 128), F32),
        pltpu.VMEM((2, 128, 2048), BF16),
        pltpu.VMEM((8, 8, 128), F32),
        pltpu.VMEM((64, 128), F32),
        pltpu.VMEM((CHUNKS, 2) + chunk, BF16),
        pltpu.VMEM((CHUNKS,) + chunk, BF16),
        pltpu.VMEM((CHUNKS, 15) + tile, BF16),
        pltpu.VMEM((CHUNKS, 2) + chunk, BF16),
        pltpu.VMEM((128, 2048), BF16),
        pltpu.VMEM((128, 2048), F32),
        pltpu.VMEM((2, 64, 2) + tile, BF16),
        pltpu.VMEM((2, 2, 64) + tile, BF16),
        pltpu.VMEM((2, 64) + tile, BF16),
        pltpu.VMEM((2, 512, 512), BF16),
        pltpu.VMEM(tile, F32),
        pltpu.VMEM((8,) + tile, F32),
        *[pltpu.VMEM((3,) + REST[axis] + tile, BF16) for axis in FIRST_AXIS],
        *[pltpu.VMEM(REST[axis] + tile, BF16) for axis in FIRST_AXIS],
        pltpu.SemaphoreType.DMA((2,)),
        pltpu.SemaphoreType.DMA((8,)),
        pltpu.SemaphoreType.DMA((10,)),
        pltpu.SemaphoreType.DMA((10,)),
        pltpu.SemaphoreType.DMA((CHUNKS * 6,)),
        pltpu.SemaphoreType.DMA((CHUNKS * 6,)),
    ]
    advanced, log_importance = pl.pallas_call(
        kernel,
        out_shape=(
            jax.ShapeDtypeStruct(walkers.shape, F32),
            jax.ShapeDtypeStruct((2,), F32),
        ),
        in_specs=[whole, whole, vmem, vmem, whole],
        out_specs=(vmem, pl.BlockSpec(memory_space=pltpu.SMEM)),
        scratch_shapes=scratch,
        compiler_params=pltpu.CompilerParams(
            collective_id=0, has_side_effects=True, vmem_limit_bytes=62 * 1024 * 1024
        ),
    )(walkers, inverse_intersection, trial, fields, cholesky)
    smem = pl.BlockSpec(memory_space=pltpu.SMEM)
    return pl.pallas_call(
        settle,
        out_shape=(
            jax.ShapeDtypeStruct(walkers.shape, F32),
            jax.ShapeDtypeStruct((2,), F32),
        ),
        in_specs=[vmem, smem],
        out_specs=(vmem, smem),
    )(advanced, log_importance)


def solution(mesh):
    in_specs = (
        P(("walk", "pair"), None, None),
        P(("walk", "pair"), None, None),
        P(None, "walk"),
        P(("walk", "pair"), None),
        P("pair", "walk", None),
    )
    out_specs = (P(("walk", "pair"), None, None), P(("walk", "pair")))
    return jax.shard_map(
        per_device, mesh=mesh, in_specs=in_specs, out_specs=out_specs, check_vma=False
    )
```

```python
import functools

import jax
import jax.numpy as jnp
from jax import lax
from jax.experimental import pallas as pl
from jax.experimental.pallas import tpu as pltpu
from jax.sharding import PartitionSpec as P

MESH = pl.DeviceIdType.MESH
F32 = jnp.float32
BF16 = jnp.bfloat16
time_root = 0.1
CHUNKS = 4
STAGES = 3
FARTHEST = sorted(range(1, 16), key=lambda i: -min(i // 4, 4 - i // 4) - min(i % 4, 4 - i % 4))
FIRST_AXIS = ("x", "y", "x", "y")
REST = {"x": (4, 2, 2), "y": (2, 4, 2), "z": (4, 4)}


def device_of(pos):
    x, y, zh, zl, c = pos
    return (x * 2 + zl, (y * 2 + zh) * 2 + c)


def moved(pos, axis, d):
    x, y, zh, zl, c = pos
    if axis == "x":
        return (lax.rem(x + d, 4), y, zh, zl, c)
    if axis == "y":
        return (x, lax.rem(y + d, 4), zh, zl, c)
    z = lax.rem(zh * 2 + zl + d, 4)
    return (x, y, z // 2, lax.rem(z, 2), c)


def slab_index(axis, pos):
    x, y, zh, zl, _ = pos
    every = slice(None)
    return {"x": (every, every, x), "y": (y,), "z": (every, zh, every, zl)}[axis]


def tile_index(axis, pos):
    x, y, zh, zl, _ = pos
    return {"x": (y, zh, zl), "y": (zh, x, zl), "z": (y, x)}[axis]


def kernel(
    walkers_in, inverse_in, trial, fields, cholesky, out, log_out,
    walkers, inverse, stage, half, turned, diag, send_a, recv_a, pass_a, wide, left, fields_out, fields_in,
    parts, from_core, sums, shifted, moved_fields, total, send_d, recv_d, pass_d, potential,
    logs, logs_in, *rest,
):
    first_in = rest[:CHUNKS]
    first_sum = rest[CHUNKS : 2 * CHUNKS]
    in_sem, slab_sem, send_sem, recv_sem, hop_send, hop_recv = rest[2 * CHUNKS :]
    a, b = lax.axis_index("walk"), lax.axis_index("pair")
    x, zl = a // 2, lax.rem(a, 2)
    c = lax.rem(b, 2)
    y, zh = b // 4, lax.rem(b // 2, 2)
    here = (x, y, zh, zl, c)
    sibling = (x, y, zh, zl, 1 - c)

    def chip_of(pos):
        return (pos[1] * 2 + pos[2]) * 8 + pos[0] * 2 + pos[3]

    chip = chip_of(here)

    xs = [lax.rem(x + d, 4) for d in range(4)]
    ys = [lax.rem(y + d, 4) for d in range(4)]
    zs = [lax.rem(zh * 2 + zl + d, 4) for d in range(4)]
    far = [
        (xs[i % 4], ys[i // 4 % 4], zs[i // 16] // 2, lax.rem(zs[i // 16], 2), c)
        for i in range(64)
    ]

    def walk_peer(i):
        return (lax.rem(x + i // 2, 4), y, zh, lax.rem(zl + i, 2), c)

    def plane_peer(axis, i):
        one, two = i // 4, i % 4
        dx, dy, dz = {"x": (0, one, two), "y": (two, 0, one), "z": (one, two, 0)}[axis]
        return far[dx + dy * 4 + dz * 16]

    def send(src, dst, sems, pos):
        pltpu.make_async_remote_copy(
            src_ref=src, dst_ref=dst, send_sem=sems[0], recv_sem=sems[1],
            device_id=device_of(pos), device_id_type=MESH,
        ).start()

    def wait(ref, sem):
        pltpu.make_async_copy(ref, ref, sem).wait()

    def pair_sems(i):
        return send_sem.at[i], recv_sem.at[i]

    def hop(n, step):
        return hop_send.at[n * 6 + step], hop_recv.at[n * 6 + step]

    def load(g):
        for q in range(4):
            pltpu.make_async_copy(
                cholesky.at[(q % 2) * 16 + g * 2 + q // 2],
                stage.at[lax.rem(g, STAGES), pl.ds(q * 64, 64)],
                slab_sem.at[g],
            ).start()

    barrier = pltpu.get_barrier_semaphore()
    pl.semaphore_signal(barrier, inc=1, device_id=device_of(sibling), device_id_type=MESH)
    pltpu.make_async_copy(walkers_in, walkers, in_sem.at[0]).start()
    pltpu.make_async_copy(inverse_in, inverse, in_sem.at[1]).start()
    for i in range(1, 64):
        pl.semaphore_signal(
            barrier, inc=1, device_id=device_of(far[i * 37 % 64]), device_id_type=MESH
        )

    def rotate(k):
        flipped = jnp.transpose(walkers[k])
        rotated = jnp.dot(
            flipped, inverse[k], precision=lax.Precision.HIGHEST, preferred_element_type=F32
        )
        rotated = rotated.reshape(16, 2, 16, 64)
        rotated = jnp.concatenate([rotated[:, 0], rotated[:, 1]], axis=-1).astype(BF16)
        send_a[k] = rotated.reshape(8, 2, 16, 128)

    def give_rotated(k):
        for i in range(1, 64):
            pos = far[i * 37 % 64]
            src = send_a.at[k, pos[1] * 2 + pos[2]]
            send(src, recv_a.at[k, :, chip], pair_sems(k), pos)
        recv_a[k, :, chip] = send_a[k, y * 2 + zh]

    for g in range(STAGES):
        load(jnp.int32(g))
    wait(walkers, in_sem.at[0])
    wait(inverse, in_sem.at[1])
    rotate(0)
    pl.semaphore_wait(barrier, 64)
    give_rotated(0)
    rotate(1)
    give_rotated(1)

    for k in range(2):
        for to in range(8):
            for lane in range(4):
                at = (lane // 2) * 2048 + to * 256 + (lane % 2) * 128
                fields_out[to, pl.ds(k * 4 + lane, 1), :] = fields[pl.ds(k, 1), pl.ds(at, 128)]
    mine = pl.ds(pl.multiple_of(a * 8, 8), 8)

    def send_fields(i, carry):
        pos = walk_peer(i)
        send(fields_out.at[device_of(pos)[0]], fields_in.at[mine], pair_sems(2), pos)
        return carry

    lax.fori_loop(1, 8, send_fields, 0)
    fields_in[mine] = fields_out[a]

    square = jnp.concatenate([trial[...].astype(F32)] * 4, axis=0)
    square = jnp.concatenate([square] * 4, axis=1)
    rows = lax.broadcasted_iota(jnp.int32, (256, 256), 0) // 64
    cols = lax.broadcasted_iota(jnp.int32, (256, 256), 1) // 64
    diag[...] = jnp.where(rows == cols, square, 0.0).astype(BF16)

    def turn(g, carry):
        block = pl.ds(pl.multiple_of(g * 256, 256), 256)
        now = lax.rem(g, STAGES)
        wait(stage.at[now], slab_sem.at[g])
        half[block] = jnp.dot(diag[...], stage[now], preferred_element_type=F32).astype(BF16)
        turned[:, block] = jnp.transpose(stage[now])

        @pl.when(g + STAGES < 8)
        def _():
            load(g + STAGES)

        return carry

    lax.fori_loop(0, 8, turn, 0)

    def regroup(k, side, source):
        def some(g, carry):
            base = pl.multiple_of(side * 1024 + g * 256, 256)
            wide[pl.ds(base, 256), :] = source[pl.ds(g * 16, 16)].astype(F32).reshape(256, 128)
            for j in range(16):
                left[
                    k, pl.ds(pl.multiple_of(side * 64 + g * 16, 16), 16), pl.ds(j * 128, 128)
                ] = wide[pl.ds(base + j, 16, stride=16), :].astype(BF16)
            return carry

        lax.fori_loop(0, 4, some, 0)

    def receive(k):
        wait(recv_a.at[k, :, pl.ds(0, 63)], recv_sem.at[k])
        send(recv_a.at[k, 1 - c], pass_a.at[k], pair_sems(3 + k), sibling)
        regroup(k, 0, recv_a.at[k, c])
        wait(pass_a.at[k], recv_sem.at[3 + k])
        regroup(k, 1, pass_a.at[k])

    def bias_chunk(n):
        got = jnp.dot(
            left[n // 2], half[:, pl.ds((n % 2) * 2048, 2048)], preferred_element_type=F32
        )
        for group in range(16):
            for to in range(8):
                tile = [
                    got[group * 8 : group * 8 + 8, at * 128 : at * 128 + 128]
                    for at in (to * 2, to * 2 + 1)
                ]
                parts[n, group // 8, (group // 2) % 4, group % 2, to // 2, to % 2] = (
                    jnp.concatenate(tile, axis=0).astype(BF16)
                )
        send(parts.at[n, 1], from_core.at[n], hop(n, 0), sibling)

    def add_core(n):
        wait(from_core.at[n], hop_recv.at[n * 6])

        def add(i, carry):
            both = parts[n, 0, i].astype(F32) + from_core[n, i].astype(F32)
            parts[n, 0, i] = both.astype(BF16)
            return carry

        lax.fori_loop(0, 4, add, 0)
        axis = FIRST_AXIS[n]
        for d in (2, 1, 3):
            pos = moved(here, axis, d)
            src = parts.at[(n, 0) + slab_index(axis, pos)]
            send(src, first_in[n].at[d - 1], hop(n, 1), pos)

    def add_first(n):
        axis = FIRST_AXIS[n]
        wait(first_in[n], hop_recv.at[n * 6 + 1])
        got = parts[(n, 0) + slab_index(axis, here)].astype(F32)
        for d in range(3):
            got = got + first_in[n][d].astype(F32)
        first_sum[n][...] = got.astype(BF16)

        for i in FARTHEST:
            pos = plane_peer(axis, i)
            send(first_sum[n].at[tile_index(axis, pos)], sums.at[n, i - 1], hop(n, 2), pos)

    def shift(n):
        axis = FIRST_AXIS[n]
        if n == 0:
            wait(fields_in.at[pl.ds(0, 56)], recv_sem.at[2])
        wait(sums.at[n], hop_recv.at[n * 6 + 2])
        bias = first_sum[n][tile_index(axis, here)].astype(F32)
        for i in range(15):
            bias = bias + sums[n, i].astype(F32)
        bias_shift = -time_root * bias
        field = jnp.concatenate(
            [fields_in[pl.ds(n * 2 + lane, 8, stride=8), :] for lane in range(2)], axis=0
        )
        place = (n, 0, y, zh, x, zl)
        shifted[place] = (field - bias_shift).astype(BF16)

        for i in FARTHEST:
            send(shifted.at[place], shifted.at[place], hop(n, 3), plane_peer(axis, i))
        term = field * bias_shift - 0.5 * bias_shift * bias_shift
        term = term[:8] + term[8:]
        rows = pl.ds((n // 2) * 8, 8)
        logs[rows] = term if n % 2 == 0 else logs[rows] + term
        if n == CHUNKS - 1:
            logs_in[a] = logs[...]

            def give_logs(i, carry):
                send(logs, logs_in.at[a], pair_sems(5), walk_peer(i))
                return carry

            lax.fori_loop(1, 8, give_logs, 0)

    def spread_plane(n):
        axis = FIRST_AXIS[n]
        wait(sums.at[n], hop_recv.at[n * 6 + 3])
        part = shifted.at[(n, 0) + slab_index(axis, here)]
        for d in (2, 1, 3):
            send(part, part, hop(n, 4), moved(here, axis, d))

    def spread_core(n):
        wait(first_in[n], hop_recv.at[n * 6 + 4])
        send(shifted.at[n, 0], shifted.at[n, 1], hop(n, 5), sibling)

    def potential_chunk(n):
        wait(shifted.at[n, 1], hop_recv.at[n * 6 + 5])
        for at in range(8):
            tiles = shifted[n, :, :, :, at // 2, at % 2].astype(F32).reshape(16, 16, 128)
            for lane in range(2):
                moved_fields[:, pl.ds((at * 2 + lane) * 128, 128)] = (
                    tiles[:, lane * 8 : lane * 8 + 8].reshape(128, 128).astype(BF16)
                )
        got = jnp.dot(
            moved_fields[...], turned[pl.ds((n % 2) * 2048, 2048)], preferred_element_type=F32
        )
        if n % 2 == 0:
            total[...] = got
        else:
            got = got + total[...]
            for j in range(16):
                wide[pl.ds(j, 128, stride=16), :] = got[:, j * 128 : j * 128 + 128]

    def give_potential(k):
        for side in range(2):

            def narrow(g, carry, side=side):
                block = wide[pl.ds(pl.multiple_of(side * 1024 + g * 256, 256), 256), :]
                send_d[k, pl.ds(g * 16, 16), side] = block.astype(BF16).reshape(16, 16, 128)
                return carry

            lax.fori_loop(0, 4, narrow, 0)

        for i in range(1, 64):
            pos = far[i * 37 % 64]
            send(send_d.at[k, chip_of(pos)], recv_d.at[k, :, chip], pair_sems(6 + k), pos)
        recv_d[k, :, chip] = send_d[k, chip]

    def pass_potential(k):
        wait(recv_d.at[k, :, pl.ds(0, 63)], recv_sem.at[6 + k])
        send(recv_d.at[k, 1], pass_d.at[k], pair_sems(8 + k), sibling)

    def assemble(k, core, source):
        def some(i, carry):
            for h in range(2):
                row = pl.multiple_of((i * 2 + core) * 32 + h * 16, 16)
                for pair in range(4):
                    both = [
                        source[i * 8 + pair * 2 + e].astype(F32)[:, h * 64 : h * 64 + 64]
                        for e in range(2)
                    ]
                    potential[k, pl.ds(row, 16), pl.ds(pair * 128, 128)] = jnp.concatenate(
                        both, axis=1
                    ).astype(BF16)
            return carry

        lax.fori_loop(0, 8, some, 0)

    def propagate(k):
        assemble(k, c, recv_d.at[k, 0])
        wait(pass_d.at[k], recv_sem.at[8 + k])
        assemble(k, 1 - c, pass_d.at[k])
        series_term = walkers[k]
        summed = series_term
        for degree in range(1, 7):
            product = lax.dot_general(
                series_term.astype(BF16), potential[k], (((1,), (1,)), ((), ())),
                preferred_element_type=F32,
            )
            series_term = product * (-time_root / degree)
            summed = summed + series_term
        out[k] = summed

    receive(0)
    bias_chunk(0)
    bias_chunk(1)
    add_core(0)
    add_core(1)
    receive(1)
    bias_chunk(2)
    bias_chunk(3)
    add_first(0)
    add_first(1)
    add_core(2)
    add_core(3)
    shift(0)
    shift(1)
    add_first(2)
    add_first(3)
    spread_plane(0)
    spread_plane(1)
    shift(2)
    shift(3)
    spread_core(0)
    spread_core(1)
    spread_plane(2)
    spread_plane(3)
    potential_chunk(0)
    potential_chunk(1)
    give_potential(0)
    spread_core(2)
    spread_core(3)
    potential_chunk(2)
    potential_chunk(3)
    give_potential(1)
    pass_potential(0)
    propagate(0)

    wait(logs_in.at[pl.ds(0, 7)], recv_sem.at[5])
    all_logs = logs_in[0]
    for i in range(1, 8):
        all_logs = all_logs + logs_in[i]
    log_rows = lax.broadcasted_iota(jnp.int32, (16, 128), 0)
    for k in range(2):
        log_out[k] = jnp.sum(jnp.where(log_rows == k * 8 + a, all_logs, 0.0))

    pass_potential(1)
    propagate(1)

    for k in range(2):
        wait(recv_a.at[k, :, pl.ds(0, 63)], send_sem.at[k])
        wait(recv_d.at[k, :, pl.ds(0, 63)], send_sem.at[6 + k])
        wait(pass_a.at[k], send_sem.at[3 + k])
        wait(pass_d.at[k], send_sem.at[8 + k])
    wait(fields_in.at[pl.ds(0, 56)], send_sem.at[2])
    wait(logs_in.at[pl.ds(0, 7)], send_sem.at[5])
    for n in range(CHUNKS):
        for step, size in enumerate(
            (from_core.at[n], first_in[n], sums.at[n], sums.at[n], first_in[n], from_core.at[n])
        ):
            wait(size, hop_send.at[n * 6 + step])


def settle(result, log, out, log_out):
    out[...] = result[...]
    for k in range(2):
        log_out[k] = log[k]


def per_device(walkers, inverse_intersection, trial, fields, cholesky):
    vmem = pl.BlockSpec(memory_space=pltpu.VMEM)
    whole = pl.BlockSpec(memory_space=pl.ANY)
    tile = (16, 128)
    chunk = (4, 2, 4, 2) + tile
    scratch = [
        pltpu.VMEM(walkers.shape, F32),
        pltpu.VMEM(inverse_intersection.shape, F32),
        pltpu.VMEM((STAGES, 256, 4096), BF16),
        pltpu.VMEM((2048, 4096), BF16),
        pltpu.VMEM((4096, 2048), BF16),
        pltpu.VMEM((256, 256), BF16),
        pltpu.VMEM((2, 8, 2) + tile, BF16),
        pltpu.VMEM((2, 2, 64) + tile, BF16),
        pltpu.VMEM((2, 64) + tile, BF16),
        pltpu.VMEM((2048, 128), F32),
        pltpu.VMEM((2, 128, 2048), BF16),
        pltpu.VMEM((8, 8, 128), F32),
        pltpu.VMEM((64, 128), F32),
        pltpu.VMEM((CHUNKS, 2) + chunk, BF16),
        pltpu.VMEM((CHUNKS,) + chunk, BF16),
        pltpu.VMEM((CHUNKS, 15) + tile, BF16),
        pltpu.VMEM((CHUNKS, 2) + chunk, BF16),
        pltpu.VMEM((128, 2048), BF16),
        pltpu.VMEM((128, 2048), F32),
        pltpu.VMEM((2, 64, 2) + tile, BF16),
        pltpu.VMEM((2, 2, 64) + tile, BF16),
        pltpu.VMEM((2, 64) + tile, BF16),
        pltpu.VMEM((2, 512, 512), BF16),
        pltpu.VMEM(tile, F32),
        pltpu.VMEM((8,) + tile, F32),
        *[pltpu.VMEM((3,) + REST[axis] + tile, BF16) for axis in FIRST_AXIS],
        *[pltpu.VMEM(REST[axis] + tile, BF16) for axis in FIRST_AXIS],
        pltpu.SemaphoreType.DMA((2,)),
        pltpu.SemaphoreType.DMA((8,)),
        pltpu.SemaphoreType.DMA((10,)),
        pltpu.SemaphoreType.DMA((10,)),
        pltpu.SemaphoreType.DMA((CHUNKS * 6,)),
        pltpu.SemaphoreType.DMA((CHUNKS * 6,)),
    ]
    advanced, log_importance = pl.pallas_call(
        kernel,
        out_shape=(
            jax.ShapeDtypeStruct(walkers.shape, F32),
            jax.ShapeDtypeStruct((2,), F32),
        ),
        in_specs=[whole, whole, vmem, vmem, whole],
        out_specs=(vmem, pl.BlockSpec(memory_space=pltpu.SMEM)),
        scratch_shapes=scratch,
        compiler_params=pltpu.CompilerParams(
            collective_id=0, has_side_effects=True, vmem_limit_bytes=62 * 1024 * 1024
        ),
    )(walkers, inverse_intersection, trial, fields, cholesky)
    smem = pl.BlockSpec(memory_space=pltpu.SMEM)
    return pl.pallas_call(
        settle,
        out_shape=(
            jax.ShapeDtypeStruct(walkers.shape, F32),
            jax.ShapeDtypeStruct((2,), F32),
        ),
        in_specs=[vmem, smem],
        out_specs=(vmem, smem),
    )(advanced, log_importance)


def solution(mesh):
    in_specs = (
        P(("walk", "pair"), None, None),
        P(("walk", "pair"), None, None),
        P(None, "walk"),
        P(("walk", "pair"), None),
        P("pair", "walk", None),
    )
    out_specs = (P(("walk", "pair"), None, None), P(("walk", "pair")))
    return jax.shard_map(
        per_device, mesh=mesh, in_specs=in_specs, out_specs=out_specs, check_vma=False
    )
```

```python
import functools

import jax
import jax.numpy as jnp
from jax import lax
from jax.experimental import pallas as pl
from jax.experimental.pallas import tpu as pltpu
from jax.sharding import PartitionSpec as P

MESH = pl.DeviceIdType.MESH
F32 = jnp.float32
BF16 = jnp.bfloat16
time_root = 0.1
CHUNKS = 4
STAGES = 3
FARTHEST = sorted(range(1, 16), key=lambda i: -min(i // 4, 4 - i // 4) - min(i % 4, 4 - i % 4))
FIRST_AXIS = ("x", "y", "x", "y")
REST = {"x": (4, 2, 2), "y": (2, 4, 2), "z": (4, 4)}


def device_of(pos):
    x, y, zh, zl, c = pos
    return (x * 2 + zl, (y * 2 + zh) * 2 + c)


def moved(pos, axis, d):
    x, y, zh, zl, c = pos
    if axis == "x":
        return (lax.rem(x + d, 4), y, zh, zl, c)
    if axis == "y":
        return (x, lax.rem(y + d, 4), zh, zl, c)
    z = lax.rem(zh * 2 + zl + d, 4)
    return (x, y, z // 2, lax.rem(z, 2), c)


def slab_index(axis, pos):
    x, y, zh, zl, _ = pos
    every = slice(None)
    return {"x": (every, every, x), "y": (y,), "z": (every, zh, every, zl)}[axis]


def tile_index(axis, pos):
    x, y, zh, zl, _ = pos
    return {"x": (y, zh, zl), "y": (zh, x, zl), "z": (y, x)}[axis]


def kernel(
    walkers_in, inverse_in, trial, fields, cholesky, out, log_out,
    walkers, inverse, stage, half, turned, diag, send_a, recv_a, pass_a, wide, left, fields_out, fields_in,
    parts, from_core, sums, shifted, moved_fields, total, send_d, recv_d, pass_d, potential,
    logs, logs_in, *rest,
):
    first_in = rest[:CHUNKS]
    first_sum = rest[CHUNKS : 2 * CHUNKS]
    in_sem, slab_sem, send_sem, recv_sem, hop_send, hop_recv = rest[2 * CHUNKS :]
    a, b = lax.axis_index("walk"), lax.axis_index("pair")
    x, zl = a // 2, lax.rem(a, 2)
    c = lax.rem(b, 2)
    y, zh = b // 4, lax.rem(b // 2, 2)
    here = (x, y, zh, zl, c)
    sibling = (x, y, zh, zl, 1 - c)

    def chip_of(pos):
        return (pos[1] * 2 + pos[2]) * 8 + pos[0] * 2 + pos[3]

    chip = chip_of(here)

    xs = [lax.rem(x + d, 4) for d in range(4)]
    ys = [lax.rem(y + d, 4) for d in range(4)]
    zs = [lax.rem(zh * 2 + zl + d, 4) for d in range(4)]
    far = [
        (xs[i % 4], ys[i // 4 % 4], zs[i // 16] // 2, lax.rem(zs[i // 16], 2), c)
        for i in range(64)
    ]

    def walk_peer(i):
        return (lax.rem(x + i // 2, 4), y, zh, lax.rem(zl + i, 2), c)

    def plane_peer(axis, i):
        one, two = i // 4, i % 4
        dx, dy, dz = {"x": (0, one, two), "y": (two, 0, one), "z": (one, two, 0)}[axis]
        return far[dx + dy * 4 + dz * 16]

    def send(src, dst, sems, pos):
        pltpu.make_async_remote_copy(
            src_ref=src, dst_ref=dst, send_sem=sems[0], recv_sem=sems[1],
            device_id=device_of(pos), device_id_type=MESH,
        ).start()

    def wait(ref, sem):
        pltpu.make_async_copy(ref, ref, sem).wait()

    def pair_sems(i):
        return send_sem.at[i], recv_sem.at[i]

    def hop(n, step):
        return hop_send.at[n * 6 + step], hop_recv.at[n * 6 + step]

    def load(g):
        for q in range(4):
            pltpu.make_async_copy(
                cholesky.at[(q % 2) * 16 + g * 2 + q // 2],
                stage.at[lax.rem(g, STAGES), pl.ds(q * 64, 64)],
                slab_sem.at[g],
            ).start()

    barrier = pltpu.get_barrier_semaphore()
    pl.semaphore_signal(barrier, inc=1, device_id=device_of(sibling), device_id_type=MESH)
    pltpu.make_async_copy(walkers_in, walkers, in_sem.at[0]).start()
    pltpu.make_async_copy(inverse_in, inverse, in_sem.at[1]).start()
    for i in range(1, 64):
        pl.semaphore_signal(
            barrier, inc=1, device_id=device_of(far[i * 37 % 64]), device_id_type=MESH
        )

    def rotate(k):
        flipped = jnp.transpose(walkers[k])
        rotated = jnp.dot(
            flipped, inverse[k], precision=lax.Precision.HIGHEST, preferred_element_type=F32
        )
        rotated = rotated.reshape(16, 2, 16, 64)
        rotated = jnp.concatenate([rotated[:, 0], rotated[:, 1]], axis=-1).astype(BF16)
        send_a[k] = rotated.reshape(8, 2, 16, 128)

    def give_rotated(k):
        for i in range(1, 64):
            pos = far[i * 37 % 64]
            src = send_a.at[k, pos[1] * 2 + pos[2]]
            send(src, recv_a.at[k, :, chip], pair_sems(k), pos)
        recv_a[k, :, chip] = send_a[k, y * 2 + zh]

    wait(walkers, in_sem.at[0])
    wait(inverse, in_sem.at[1])
    rotate(0)
    pl.semaphore_wait(barrier, 64)
    give_rotated(0)
    for g in range(STAGES):
        load(jnp.int32(g))
    rotate(1)
    give_rotated(1)

    for k in range(2):
        for to in range(8):
            for lane in range(4):
                at = (lane // 2) * 2048 + to * 256 + (lane % 2) * 128
                fields_out[to, pl.ds(k * 4 + lane, 1), :] = fields[pl.ds(k, 1), pl.ds(at, 128)]
    mine = pl.ds(pl.multiple_of(a * 8, 8), 8)

    def send_fields(i, carry):
        pos = walk_peer(i)
        send(fields_out.at[device_of(pos)[0]], fields_in.at[mine], pair_sems(2), pos)
        return carry

    lax.fori_loop(1, 8, send_fields, 0)
    fields_in[mine] = fields_out[a]

    square = jnp.concatenate([trial[...].astype(F32)] * 4, axis=0)
    square = jnp.concatenate([square] * 4, axis=1)
    rows = lax.broadcasted_iota(jnp.int32, (256, 256), 0) // 64
    cols = lax.broadcasted_iota(jnp.int32, (256, 256), 1) // 64
    diag[...] = jnp.where(rows == cols, square, 0.0).astype(BF16)

    def turn(g, carry):
        block = pl.ds(pl.multiple_of(g * 256, 256), 256)
        now = lax.rem(g, STAGES)
        wait(stage.at[now], slab_sem.at[g])
        half[block] = jnp.dot(diag[...], stage[now], preferred_element_type=F32).astype(BF16)
        turned[:, block] = jnp.transpose(stage[now])

        @pl.when(g + STAGES < 8)
        def _():
            load(g + STAGES)

        return carry

    lax.fori_loop(0, 8, turn, 0)

    def regroup(k, side, source):
        def some(g, carry):
            base = pl.multiple_of(side * 1024 + g * 256, 256)
            wide[pl.ds(base, 256), :] = source[pl.ds(g * 16, 16)].astype(F32).reshape(256, 128)
            for j in range(16):
                left[
                    k, pl.ds(pl.multiple_of(side * 64 + g * 16, 16), 16), pl.ds(j * 128, 128)
                ] = wide[pl.ds(base + j, 16, stride=16), :].astype(BF16)
            return carry

        lax.fori_loop(0, 4, some, 0)

    def receive(k):
        wait(recv_a.at[k, :, pl.ds(0, 63)], recv_sem.at[k])
        send(recv_a.at[k, 1 - c], pass_a.at[k], pair_sems(3 + k), sibling)
        regroup(k, 0, recv_a.at[k, c])
        wait(pass_a.at[k], recv_sem.at[3 + k])
        regroup(k, 1, pass_a.at[k])

    def bias_chunk(n):
        got = jnp.dot(
            left[n // 2], half[:, pl.ds((n % 2) * 2048, 2048)], preferred_element_type=F32
        )
        for group in range(16):
            for to in range(8):
                tile = [
                    got[group * 8 : group * 8 + 8, at * 128 : at * 128 + 128]
                    for at in (to * 2, to * 2 + 1)
                ]
                parts[n, group // 8, (group // 2) % 4, group % 2, to // 2, to % 2] = (
                    jnp.concatenate(tile, axis=0).astype(BF16)
                )
        send(parts.at[n, 1], from_core.at[n], hop(n, 0), sibling)

    def add_core(n):
        wait(from_core.at[n], hop_recv.at[n * 6])

        def add(i, carry):
            both = parts[n, 0, i].astype(F32) + from_core[n, i].astype(F32)
            parts[n, 0, i] = both.astype(BF16)
            return carry

        lax.fori_loop(0, 4, add, 0)
        axis = FIRST_AXIS[n]
        for d in (2, 1, 3):
            pos = moved(here, axis, d)
            src = parts.at[(n, 0) + slab_index(axis, pos)]
            send(src, first_in[n].at[d - 1], hop(n, 1), pos)

    def add_first(n):
        axis = FIRST_AXIS[n]
        wait(first_in[n], hop_recv.at[n * 6 + 1])
        got = parts[(n, 0) + slab_index(axis, here)].astype(F32)
        for d in range(3):
            got = got + first_in[n][d].astype(F32)
        first_sum[n][...] = got.astype(BF16)

        for i in FARTHEST:
            pos = plane_peer(axis, i)
            send(first_sum[n].at[tile_index(axis, pos)], sums.at[n, i - 1], hop(n, 2), pos)

    def shift(n):
        axis = FIRST_AXIS[n]
        if n == 0:
            wait(fields_in.at[pl.ds(0, 56)], recv_sem.at[2])
        wait(sums.at[n], hop_recv.at[n * 6 + 2])
        bias = first_sum[n][tile_index(axis, here)].astype(F32)
        for i in range(15):
            bias = bias + sums[n, i].astype(F32)
        bias_shift = -time_root * bias
        field = jnp.concatenate(
            [fields_in[pl.ds(n * 2 + lane, 8, stride=8), :] for lane in range(2)], axis=0
        )
        place = (n, 0, y, zh, x, zl)
        shifted[place] = (field - bias_shift).astype(BF16)

        for i in FARTHEST:
            send(shifted.at[place], shifted.at[place], hop(n, 3), plane_peer(axis, i))
        term = field * bias_shift - 0.5 * bias_shift * bias_shift
        term = term[:8] + term[8:]
        rows = pl.ds((n // 2) * 8, 8)
        logs[rows] = term if n % 2 == 0 else logs[rows] + term
        if n == CHUNKS - 1:
            logs_in[a] = logs[...]

            def give_logs(i, carry):
                send(logs, logs_in.at[a], pair_sems(5), walk_peer(i))
                return carry

            lax.fori_loop(1, 8, give_logs, 0)

    def spread_plane(n):
        axis = FIRST_AXIS[n]
        wait(sums.at[n], hop_recv.at[n * 6 + 3])
        part = shifted.at[(n, 0) + slab_index(axis, here)]
        for d in (2, 1, 3):
            send(part, part, hop(n, 4), moved(here, axis, d))

    def spread_core(n):
        wait(first_in[n], hop_recv.at[n * 6 + 4])
        send(shifted.at[n, 0], shifted.at[n, 1], hop(n, 5), sibling)

    def potential_chunk(n):
        wait(shifted.at[n, 1], hop_recv.at[n * 6 + 5])
        for at in range(8):
            tiles = shifted[n, :, :, :, at // 2, at % 2].astype(F32).reshape(16, 16, 128)
            for lane in range(2):
                moved_fields[:, pl.ds((at * 2 + lane) * 128, 128)] = (
                    tiles[:, lane * 8 : lane * 8 + 8].reshape(128, 128).astype(BF16)
                )
        got = jnp.dot(
            moved_fields[...], turned[pl.ds((n % 2) * 2048, 2048)], preferred_element_type=F32
        )
        if n % 2 == 0:
            total[...] = got
        else:
            got = got + total[...]
            for j in range(16):
                wide[pl.ds(j, 128, stride=16), :] = got[:, j * 128 : j * 128 + 128]

    def give_potential(k):
        for side in range(2):

            def narrow(g, carry, side=side):
                block = wide[pl.ds(pl.multiple_of(side * 1024 + g * 256, 256), 256), :]
                send_d[k, pl.ds(g * 16, 16), side] = block.astype(BF16).reshape(16, 16, 128)
                return carry

            lax.fori_loop(0, 4, narrow, 0)

        for i in range(1, 64):
            pos = far[i * 37 % 64]
            send(send_d.at[k, chip_of(pos)], recv_d.at[k, :, chip], pair_sems(6 + k), pos)
        recv_d[k, :, chip] = send_d[k, chip]

    def pass_potential(k):
        wait(recv_d.at[k, :, pl.ds(0, 63)], recv_sem.at[6 + k])
        send(recv_d.at[k, 1], pass_d.at[k], pair_sems(8 + k), sibling)

    def assemble(k, core, source):
        def some(i, carry):
            for h in range(2):
                row = pl.multiple_of((i * 2 + core) * 32 + h * 16, 16)
                for pair in range(4):
                    both = [
                        source[i * 8 + pair * 2 + e].astype(F32)[:, h * 64 : h * 64 + 64]
                        for e in range(2)
                    ]
                    potential[k, pl.ds(row, 16), pl.ds(pair * 128, 128)] = jnp.concatenate(
                        both, axis=1
                    ).astype(BF16)
            return carry

        lax.fori_loop(0, 8, some, 0)

    def propagate(k):
        assemble(k, c, recv_d.at[k, 0])
        wait(pass_d.at[k], recv_sem.at[8 + k])
        assemble(k, 1 - c, pass_d.at[k])
        series_term = walkers[k]
        summed = series_term
        for degree in range(1, 7):
            product = lax.dot_general(
                series_term.astype(BF16), potential[k], (((1,), (1,)), ((), ())),
                preferred_element_type=F32,
            )
            series_term = product * (-time_root / degree)
            summed = summed + series_term
        out[k] = summed

    receive(0)
    bias_chunk(0)
    bias_chunk(1)
    add_core(0)
    add_core(1)
    receive(1)
    bias_chunk(2)
    bias_chunk(3)
    add_first(0)
    add_first(1)
    add_core(2)
    add_core(3)
    shift(0)
    shift(1)
    add_first(2)
    add_first(3)
    spread_plane(0)
    spread_plane(1)
    shift(2)
    shift(3)
    spread_core(0)
    spread_core(1)
    spread_plane(2)
    spread_plane(3)
    potential_chunk(0)
    potential_chunk(1)
    give_potential(0)
    spread_core(2)
    spread_core(3)
    potential_chunk(2)
    potential_chunk(3)
    give_potential(1)
    pass_potential(0)
    propagate(0)

    wait(logs_in.at[pl.ds(0, 7)], recv_sem.at[5])
    all_logs = logs_in[0]
    for i in range(1, 8):
        all_logs = all_logs + logs_in[i]
    log_rows = lax.broadcasted_iota(jnp.int32, (16, 128), 0)
    for k in range(2):
        log_out[k] = jnp.sum(jnp.where(log_rows == k * 8 + a, all_logs, 0.0))

    pass_potential(1)
    propagate(1)

    for k in range(2):
        wait(recv_a.at[k, :, pl.ds(0, 63)], send_sem.at[k])
        wait(recv_d.at[k, :, pl.ds(0, 63)], send_sem.at[6 + k])
        wait(pass_a.at[k], send_sem.at[3 + k])
        wait(pass_d.at[k], send_sem.at[8 + k])
    wait(fields_in.at[pl.ds(0, 56)], send_sem.at[2])
    wait(logs_in.at[pl.ds(0, 7)], send_sem.at[5])
    for n in range(CHUNKS):
        for step, size in enumerate(
            (from_core.at[n], first_in[n], sums.at[n], sums.at[n], first_in[n], from_core.at[n])
        ):
            wait(size, hop_send.at[n * 6 + step])


def settle(result, log, out, log_out):
    out[...] = result[...]
    for k in range(2):
        log_out[k] = log[k]


def per_device(walkers, inverse_intersection, trial, fields, cholesky):
    vmem = pl.BlockSpec(memory_space=pltpu.VMEM)
    whole = pl.BlockSpec(memory_space=pl.ANY)
    tile = (16, 128)
    chunk = (4, 2, 4, 2) + tile
    scratch = [
        pltpu.VMEM(walkers.shape, F32),
        pltpu.VMEM(inverse_intersection.shape, F32),
        pltpu.VMEM((STAGES, 256, 4096), BF16),
        pltpu.VMEM((2048, 4096), BF16),
        pltpu.VMEM((4096, 2048), BF16),
        pltpu.VMEM((256, 256), BF16),
        pltpu.VMEM((2, 8, 2) + tile, BF16),
        pltpu.VMEM((2, 2, 64) + tile, BF16),
        pltpu.VMEM((2, 64) + tile, BF16),
        pltpu.VMEM((2048, 128), F32),
        pltpu.VMEM((2, 128, 2048), BF16),
        pltpu.VMEM((8, 8, 128), F32),
        pltpu.VMEM((64, 128), F32),
        pltpu.VMEM((CHUNKS, 2) + chunk, BF16),
        pltpu.VMEM((CHUNKS,) + chunk, BF16),
        pltpu.VMEM((CHUNKS, 15) + tile, BF16),
        pltpu.VMEM((CHUNKS, 2) + chunk, BF16),
        pltpu.VMEM((128, 2048), BF16),
        pltpu.VMEM((128, 2048), F32),
        pltpu.VMEM((2, 64, 2) + tile, BF16),
        pltpu.VMEM((2, 2, 64) + tile, BF16),
        pltpu.VMEM((2, 64) + tile, BF16),
        pltpu.VMEM((2, 512, 512), BF16),
        pltpu.VMEM(tile, F32),
        pltpu.VMEM((8,) + tile, F32),
        *[pltpu.VMEM((3,) + REST[axis] + tile, BF16) for axis in FIRST_AXIS],
        *[pltpu.VMEM(REST[axis] + tile, BF16) for axis in FIRST_AXIS],
        pltpu.SemaphoreType.DMA((2,)),
        pltpu.SemaphoreType.DMA((8,)),
        pltpu.SemaphoreType.DMA((10,)),
        pltpu.SemaphoreType.DMA((10,)),
        pltpu.SemaphoreType.DMA((CHUNKS * 6,)),
        pltpu.SemaphoreType.DMA((CHUNKS * 6,)),
    ]
    advanced, log_importance = pl.pallas_call(
        kernel,
        out_shape=(
            jax.ShapeDtypeStruct(walkers.shape, F32),
            jax.ShapeDtypeStruct((2,), F32),
        ),
        in_specs=[whole, whole, vmem, vmem, whole],
        out_specs=(vmem, pl.BlockSpec(memory_space=pltpu.SMEM)),
        scratch_shapes=scratch,
        compiler_params=pltpu.CompilerParams(
            collective_id=0, has_side_effects=True, vmem_limit_bytes=62 * 1024 * 1024
        ),
    )(walkers, inverse_intersection, trial, fields, cholesky)
    smem = pl.BlockSpec(memory_space=pltpu.SMEM)
    return pl.pallas_call(
        settle,
        out_shape=(
            jax.ShapeDtypeStruct(walkers.shape, F32),
            jax.ShapeDtypeStruct((2,), F32),
        ),
        in_specs=[vmem, smem],
        out_specs=(vmem, smem),
    )(advanced, log_importance)


def solution(mesh):
    in_specs = (
        P(("walk", "pair"), None, None),
        P(("walk", "pair"), None, None),
        P(None, "walk"),
        P(("walk", "pair"), None),
        P("pair", "walk", None),
    )
    out_specs = (P(("walk", "pair"), None, None), P(("walk", "pair")))
    return jax.shard_map(
        per_device, mesh=mesh, in_specs=in_specs, out_specs=out_specs, check_vma=False
    )
```
